512 devices in a mesh: along: 16 (over z), across: 32 (over x, y, core).
Axes of the slice: x: 4, y: 4, z: 16, core: 2. Of those that a mesh axis runs over, the one named last changes fastest.
Arguments:
- toa: bfloat16 [6, 3072, 8192], P(None, 'along', 'across'), may hold values from 0.015 to 1.21
- aot_seed: float32 [96, 256], P('along', 'across'), may hold values from 0.05 to 0.8
- valid: int32 [96, 256], P('along', 'across'), may hold values 0 or 1
- cloud: int32 [96, 256], P('along', 'across'), may hold values 0 or 1
- land_class: int32 [96, 256], P('along', 'across'), may hold values from 0 to 2
- row_taps: float32 [6, 3, 201], replicated, may hold values from 0.0015 to 1.31, as said below
- col_taps: float32 [6, 3, 201], replicated, may hold values from 0.0015 to 1.31, as said below
- tau: float32 [6], replicated, may hold values from 0.4 to 1.6
- adjacency: float32 [6], replicated, may hold values from 0.5 to 1.5
Outputs:
- surface: float32 [6, 3072, 8192], P(None, 'along', 'across')
The draws below stay inside these ranges and needn't reach their ends.
Inputs may be any that keep to these rules, and one draw needn't show every extreme that they name: `row_taps`: positive taps. `col_taps`: positive taps.
All inputs are finite; a program needn't handle non-finite values. No bound on the sum of `valid` or of `cloud` on one device may be relied on, other than what follows from the above.
Results may differ from the reference program's by a relative error of at most 0.00055.
Values may be sent and summed in bfloat16 or wider, within the bound.
No kernel may reach another device: no remote copies, remote signals or barrier semaphores. Data moves between devices by JAX's collectives and lax.ppermute only.
A program may use at most 64 MiB of HBM per device.

```python
import math
import jax
import jax.numpy as jnp
from jax import lax

BANDS = 6
KR = 100
TAPS = 201
CB = 32
SWEEPS = 4
ROWS = 3072
COLS = 8192
CROWS = 96
CCOLS = 256


def draw_toa(key, part):
    base_key = jax.random.fold_in(key, 11)
    first, second, third, fourth = jax.random.split(base_key, 4)
    block = 13
    coarse_shape = (BANDS, ROWS // block + 1, COLS // block + 1)
    coarse = jax.random.uniform(first, coarse_shape, jnp.float32, 0.025, 0.25)
    bright = jax.random.uniform(third, (BANDS, ROWS, COLS), jnp.float32, 0.8, 1.2)
    coarse = jnp.repeat(jnp.repeat(coarse, block, axis=1), block, axis=2)[:, :ROWS, :COLS]
    pixel = jax.random.uniform(second, (BANDS, ROWS, COLS), jnp.float32, 0.7, 1.3)
    targets = jax.random.randint(fourth, (BANDS, ROWS, COLS), 0, 64) == 0
    field = jnp.where(targets, bright, coarse * pixel)
    return field.astype(jnp.bfloat16)


def kernel_taps(key, salt):
    base_key = jax.random.fold_in(key, salt)
    first, second, third = jax.random.split(base_key, 3)
    width = jnp.exp(jax.random.uniform(first, (BANDS, 3, 1), jnp.float32, jnp.log(1.5), jnp.log(16.0)))
    distance = jnp.abs(jnp.arange(TAPS, dtype=jnp.float32) - KR)[None, None, :]
    rough = jax.random.uniform(second, (BANDS, 3, TAPS), jnp.float32, 0.7, 1.3)
    floor = 0.003 * jax.random.uniform(third, (BANDS, 3, TAPS), jnp.float32, 0.5, 1.5)
    return jnp.exp(-distance / width) * rough + floor


def draw_row_taps(key, part):
    return kernel_taps(key, 23)


def draw_col_taps(key, part):
    return kernel_taps(key, 37)


def touch_ends(entries, rng, low, largest):
    longest = entries.shape.index(max(entries.shape))
    spots = []
    for shift in (0, 1):
        where = [jax.random.randint(jax.random.fold_in(rng, axis), (), 0, length) for axis, length in enumerate(entries.shape)]
        where[longest] = (where[longest] + shift) % entries.shape[longest]
        spots.append(tuple(where))
    return entries.at[spots[0]].set(low).at[spots[1]].set(largest)


def levels(rng, dims, cuts, smallest, high):
    def one(axis_at, parts):
        draws = jax.random.uniform(jax.random.fold_in(jax.random.fold_in(rng, 6), axis_at), (parts,), jnp.float32, smallest / len(cuts), high / len(cuts))
        return jnp.repeat(jnp.exp(draws), dims[axis_at] // parts).reshape((-1,) + (1,) * (len(dims) - axis_at - 1))

    level = one(*cuts[0])
    for cut in cuts[1:]:
        level = level * one(*cut)
    return level


def setup_inputs(seed: int = 0) -> dict:
    key_of = jax.random.split(jax.random.key(seed), 10)
    toa = draw_toa(jax.random.fold_in(key_of[9], 71), 0)
    aot_seed = jnp.clip(jnp.exp(math.log(0.8) - 2.7725887 * jax.random.uniform(key_of[1], (CROWS, CCOLS), jnp.float32) ** levels(key_of[1], (CROWS, CCOLS), ((0, 16), (1, 32)), -0.2, 0.2)), 0.05, 0.8)
    valid = touch_ends((jax.random.randint(key_of[2], (CROWS, CCOLS), 0, 2) < 1).astype(jnp.int32), jax.random.fold_in(key_of[2], 1), 0, 1)
    cloud = touch_ends((jax.random.randint(key_of[3], (CROWS, CCOLS), 0, 4) < 1).astype(jnp.int32), jax.random.fold_in(key_of[3], 1), 0, 1)
    land_class = touch_ends(jax.random.randint(key_of[4], (CROWS, CCOLS), 0, 3), jax.random.fold_in(key_of[4], 1), 0, 2).astype(jnp.int32)
    row_taps = draw_row_taps(jax.random.fold_in(key_of[9], 71), 0)
    col_taps = draw_col_taps(jax.random.fold_in(key_of[9], 71), 0)
    tau = jnp.clip(jnp.exp(jax.random.uniform(key_of[7], (BANDS,), jnp.float32, math.log(0.4), math.log(1.6))), 0.4, 1.6)
    adjacency = jnp.clip(jax.random.uniform(key_of[8], (BANDS,), jnp.float32, 0.5, 1.5), 0.5, 1.5)
    return {"toa": toa, "aot_seed": aot_seed, "valid": valid, "cloud": cloud, "land_class": land_class, "row_taps": row_taps, "col_taps": col_taps, "tau": tau, "adjacency": adjacency}


def relax(aot, fix, mult, count):
    padded = jnp.pad(aot, 1)
    near = padded[2:, 1:-1] + padded[:-2, 1:-1] + padded[1:-1, 2:] + padded[1:-1, :-2]
    return fix + mult * (near / count)


def correlate(field, taps, axis):
    length = field.shape[axis]
    total = length + 2 * KR
    spectrum = jnp.fft.rfft(field, n=total, axis=axis)
    kernel = jnp.fft.rfft(taps[::-1], n=total)
    if axis == 0:
        kernel = kernel[:, None]
    else:
        kernel = kernel[None, :]
    result = jnp.fft.irfft(spectrum * kernel, n=total, axis=axis)
    return lax.slice_in_dim(result, KR, KR + length, axis=axis)


def reference(toa, aot_seed, valid, cloud, land_class, row_taps, col_taps, tau, adjacency):
    conf = (valid * (1 - cloud)).astype(jnp.float32)
    prior = jnp.where(land_class == 0, 0.06, jnp.where(land_class == 1, 0.2, 0.45)).astype(jnp.float32)
    fix = conf * aot_seed + (1.0 - conf) * (0.3 * prior)
    mult = 0.7 * (1.0 - conf)
    aot = conf * aot_seed + (1.0 - conf) * prior
    ones_pad = jnp.pad(jnp.ones_like(aot), 1)
    count = ones_pad[2:, 1:-1] + ones_pad[:-2, 1:-1] + ones_pad[1:-1, 2:] + ones_pad[1:-1, :-2]
    for sweep in range(SWEEPS):
        aot = relax(aot, fix, mult, count)
    aot_fine = jnp.repeat(jnp.repeat(aot, CB, axis=0), CB, axis=1)
    row_norm = (row_taps / jnp.sum(row_taps, axis=-1, keepdims=True)).astype(jnp.bfloat16).astype(jnp.float32)
    col_norm = (col_taps / jnp.sum(col_taps, axis=-1, keepdims=True)).astype(jnp.bfloat16).astype(jnp.float32)
    centers = jnp.array([0.1, 0.35, 0.7], jnp.float32)
    gauss = []
    for kern in range(3):
        offset = aot_fine - centers[kern]
        gauss.append(jnp.exp(-(offset * offset) / 0.08))
    gauss_total = gauss[0] + gauss[1] + gauss[2]
    results = []
    for band in range(BANDS):
        pixels = toa[band].astype(jnp.float32)
        env = jnp.zeros_like(pixels)
        for kern in range(3):
            colpass = correlate(pixels, col_norm[band, kern], 1).astype(jnp.bfloat16)
            colpass = lax.optimization_barrier(colpass).astype(jnp.float32)
            blurred = correlate(colpass, row_norm[band, kern], 0)
            env = env + (gauss[kern] / gauss_total) * blurred
        trans = jnp.exp(-tau[band] * aot_fine)
        results.append((pixels + adjacency[band] * (pixels - env)) / trans)
    return jnp.stack(results)
```

```python
import jax
import jax.numpy as jnp
from jax import lax
from jax.experimental import pallas as pl
from jax.experimental.pallas import tpu as pltpu
from jax.sharding import PartitionSpec as P

BANDS = 6
KR = 100
TAPS = 201
CB = 32
SWEEPS = 4
ROWS = 192
COLS = 256
HALO = 104
SIDE = 128
F32 = jnp.float32
BF16 = jnp.bfloat16


def iota(shape, dim):
    return lax.broadcasted_iota(jnp.int32, shape, dim)


def shift(value, axis, step):
    count = lax.axis_size(axis)
    pairs = [(i, i + step) for i in range(count) if 0 <= i + step < count]
    return lax.ppermute(value, axis, pairs)


def toeplitz_kernel(row_ref, col_ref, row_out, col_out, pad_ref):
    pad_ref[...] = jnp.zeros_like(pad_ref)
    raw = row_ref[0]
    pad_ref[0:3, 4 : 4 + TAPS] = raw / jnp.sum(raw, axis=-1, keepdims=True)
    raw = col_ref[0]
    pad_ref[8:11, 4 : 4 + TAPS] = raw / jnp.sum(raw, axis=-1, keepdims=True)
    taps = pad_ref[...].astype(BF16)
    flip = (iota((256, 256), 0) + iota((256, 256), 1) == TAPS + 7).astype(F32).astype(BF16)
    flipped = jnp.dot(taps, flip, preferred_element_type=F32)
    taps = taps.astype(F32)
    col_index = iota((384, 128), 1) - iota((384, 128), 0) + (SIDE + KR)
    col_good = (col_index >= 0) & (col_index < TAPS)
    row_at = iota((ROWS, 256), 1)
    row_base = row_at - iota((ROWS, 256), 0)
    near = row_base + KR
    near_good = (near >= 0) & (near < TAPS)
    tail = row_base + (256 + KR)
    tail_good = (tail < TAPS) & (row_at < 40)
    above = row_base + (256 - 304 - HALO + KR)
    above_good = (above >= 0) & (above < TAPS) & (row_at >= 48) & (row_at < 152)

    def spread(vector, first):
        wide = jnp.broadcast_to(vector, (128, 256))
        return pltpu.roll(wide, first, 1, stride=1, stride_axis=0)

    def tall(value):
        swapped = jnp.concatenate([value[0:64, 128:256], value[0:64, 0:128]], axis=1)
        return jnp.concatenate([value, swapped], axis=0)

    for kern in range(3):
        rolled = spread(flipped[8 + kern : 9 + kern], 24)
        rolled = jnp.concatenate(
            [rolled[:, 0:128], rolled[:, 128:256], rolled[:, 0:128]], axis=0
        )
        tile = jnp.where(col_good, rolled, 0.0).astype(BF16)
        left = kern * COLS
        col_out[0, 0:384, left : left + 128] = tile
        col_out[0, 384:512, left : left + 128] = jnp.zeros((128, 128), BF16)
        col_out[0, 0:128, left + 128 : left + 256] = jnp.zeros((128, 128), BF16)
        col_out[0, 128:512, left + 128 : left + 256] = tile
        rolled = tall(spread(taps[kern : kern + 1], 152))
        other = tall(spread(taps[kern : kern + 1], 48))
        top = kern * ROWS
        row_out[0, top : top + ROWS, 0:256] = jnp.where(near_good, rolled, 0.0).astype(BF16)
        row_out[0, top : top + ROWS, 256:512] = jnp.where(
            tail_good, rolled, jnp.where(above_good, other, 0.0)
        ).astype(BF16)


def toeplitz(row_taps, col_taps):
    spec = pl.BlockSpec((1, 3, TAPS), lambda b: (b, 0, 0))
    return pl.pallas_call(
        toeplitz_kernel,
        grid=(BANDS,),
        in_specs=[spec, spec],
        out_specs=[
            pl.BlockSpec((1, 3 * ROWS, 512), lambda b: (b, 0, 0)),
            pl.BlockSpec((1, 512, 3 * COLS), lambda b: (b, 0, 0)),
        ],
        out_shape=[
            jax.ShapeDtypeStruct((BANDS, 3 * ROWS, 512), BF16),
            jax.ShapeDtypeStruct((BANDS, 512, 3 * COLS), BF16),
        ],
        scratch_shapes=[pltpu.VMEM((16, 256), F32)],
        cost_estimate=pl.CostEstimate(flops=0, bytes_accessed=8_000_000, transcendentals=0),
        name="toeplitz",
    )(row_taps, col_taps)


def cell_state(cells, up, down, left, right, up_left, up_right, down_left, down_right, place):
    sub = iota((8, 128), 0)
    lane = iota((8, 128), 1)
    parts = []
    for v in range(5):
        top = jnp.where(
            lane < 4,
            up_left[v, 0:8, :].astype(F32),
            jnp.where(lane < 12, up[v, 0:8, :].astype(F32), up_right[v, 0:8, :].astype(F32)),
        )
        low = jnp.where(
            lane < 4,
            down_left[v, :, :].astype(F32),
            jnp.where(lane < 12, down[v, :, :].astype(F32), down_right[v, :, :].astype(F32)),
        )
        east = pltpu.roll(right[v].astype(F32), 16, 1)
        both = iota((16, 128), 1)
        middle = jnp.where(
            both < 4,
            left[v].astype(F32),
            jnp.where(both < 12, cells[v].astype(F32), east),
        )
        first = jnp.where(sub < 6, pltpu.roll(top, 2, 0), middle[0:8])
        second = jnp.where(sub < 4, middle[8:16], low)
        parts.append(jnp.concatenate([first, second], axis=0))
    seed = parts[0] + parts[1] + parts[2]
    conf = parts[3]
    kind = parts[4]
    prior = jnp.where(kind < 0.5, 0.06, jnp.where(kind < 1.5, 0.2, 0.45))
    row = place[0] + iota((16, 128), 0) - 6
    col = place[1] + iota((16, 128), 1) - 4
    last_row = place[2] - 1
    last_col = place[3] - 1
    inside = (row >= 0) & (row <= last_row) & (col >= 0) & (col <= last_col)
    count = (
        (row > 0).astype(F32)
        + (row < last_row).astype(F32)
        + (col > 0).astype(F32)
        + (col < last_col).astype(F32)
    )
    count = jnp.maximum(count, 1.0)
    fix = conf * seed + (1.0 - conf) * (0.3 * prior)
    mult = 0.7 * (1.0 - conf)
    aot = jnp.where(inside, conf * seed + (1.0 - conf) * prior, 0.0)
    for _ in range(SWEEPS):
        near = (
            pltpu.roll(aot, 15, 0)
            + pltpu.roll(aot, 1, 0)
            + pltpu.roll(aot, 127, 1)
            + pltpu.roll(aot, 1, 1)
        )
        aot = jnp.where(inside, fix + mult * (near / count), 0.0)
    return pltpu.roll(aot, 10, 0)[0:8]


def main_kernel(
    place,
    tau,
    adjacency,
    toa,
    up,
    down,
    left,
    right,
    up_left,
    down_left,
    up_right,
    down_right,
    row_mat,
    col_mat,
    cells,
    up_c,
    down_c,
    left_c,
    right_c,
    up_left_c,
    down_left_c,
    up_right_c,
    down_right_c,
    out,
    field,
    passed,
    fine,
):
    band = pl.program_id(0)

    @pl.when(band == 0)
    def _():
        field[288:304, :] = jnp.zeros((16, 512), BF16)
        field[400:416, :] = jnp.zeros((16, 512), BF16)
        passed[416:512, :] = jnp.zeros((96, 3 * COLS), BF16)
        small = cell_state(
            cells, up_c, down_c, left_c, right_c, up_left_c, up_right_c, down_left_c,
            down_right_c, place,
        )
        block = iota((8, COLS), 1) // CB
        aot = jnp.zeros((8, COLS), F32)
        for j in range(COLS // CB):
            aot = jnp.where(block == j, small[:, 4 + j : 5 + j], aot)
        gauss = []
        for center in (0.1, 0.35, 0.7):
            offset = aot - center
            gauss.append(jnp.exp(-(offset * offset) / 0.08))
        total = gauss[0] + gauss[1] + gauss[2]
        fine[0:8, :] = aot
        for kern in range(3):
            fine[8 + 8 * kern : 16 + 8 * kern, :] = gauss[kern] / total

    field[0:ROWS, 0:128] = left[0]
    field[0:ROWS, 128:384] = toa[0]
    field[0:ROWS, 384:512] = right[0]
    field[192:296, 0:128] = down_left[0]
    field[192:296, 128:384] = down[0]
    field[192:296, 384:512] = down_right[0]
    field[304:408, 0:128] = up_left[0]
    field[304:408, 128:384] = up[0]
    field[304:408, 384:512] = up_right[0]
    passed[0:416, :] = jnp.dot(field[...], col_mat[0], preferred_element_type=F32).astype(BF16)
    growth = jnp.exp(tau[band] * fine[0:8, :])
    own = (1.0 + adjacency[band]) * growth
    scaled = adjacency[band] * growth
    envs = []
    for kern in range(3):
        envs.append(
            jnp.dot(
                row_mat[0, kern * ROWS : (kern + 1) * ROWS, :],
                passed[:, kern * COLS : (kern + 1) * COLS],
                preferred_element_type=F32,
            )
        )
    weights = [scaled * fine[8 + 8 * kern : 16 + 8 * kern, :] for kern in range(3)]
    for i in range(ROWS // CB):
        part = slice(i * CB, (i + 1) * CB)
        value = own[i : i + 1, :] * toa[0, part, :].astype(F32)
        for kern in range(3):
            value = value - weights[kern][i : i + 1, :] * envs[kern][part, :]
        out[0, part, :] = value


def correct(place, tau, adjacency, toa, up, down, left, right, from_left, from_right, row_mat, col_mat, cells):
    smem = pl.BlockSpec(memory_space=pltpu.SMEM)
    halo = pl.BlockSpec((1, HALO, COLS), lambda b: (b, 0, 0))
    side = pl.BlockSpec((1, ROWS, SIDE), lambda b: (b, 0, 0))
    corner_up = pl.BlockSpec((1, HALO, SIDE), lambda b: (b, 0, 0))
    corner_down = pl.BlockSpec((1, HALO, SIDE), lambda b: (b + BANDS, 0, 0))
    head = pl.BlockSpec((BANDS, 16, 128), lambda b: (0, 0, 0))
    foot = pl.BlockSpec((BANDS, 8, 128), lambda b: (0, 12, 0))
    foot_low = pl.BlockSpec((BANDS, 8, 128), lambda b: (1, 12, 0))
    east = pl.BlockSpec((BANDS, 16, 128), lambda b: (0, 0, 0))
    flops = BANDS * 2 * (416 * 512 * 768 + 3 * 192 * 512 * 256)
    return pl.pallas_call(
        main_kernel,
        grid=(BANDS,),
        in_specs=[
            smem,
            smem,
            smem,
            pl.BlockSpec((1, ROWS, COLS), lambda b: (b, 0, 0)),
            halo,
            halo,
            side,
            side,
            corner_up,
            corner_down,
            corner_up,
            corner_down,
            pl.BlockSpec((1, 3 * ROWS, 512), lambda b: (b, 0, 0)),
            pl.BlockSpec((1, 512, 3 * COLS), lambda b: (b, 0, 0)),
            head,
            head,
            foot,
            head,
            east,
            head,
            foot_low,
            head,
            foot_low,
        ],
        out_specs=pl.BlockSpec((1, ROWS, COLS), lambda b: (b, 0, 0)),
        out_shape=jax.ShapeDtypeStruct((BANDS, ROWS, COLS), F32),
        scratch_shapes=[
            pltpu.VMEM((416, 512), BF16),
            pltpu.VMEM((512, 3 * COLS), BF16),
            pltpu.VMEM((32, COLS), F32),
        ],
        cost_estimate=pl.CostEstimate(
            flops=flops, bytes_accessed=12_000_000, transcendentals=0
        ),
        compiler_params=pltpu.CompilerParams(vmem_limit_bytes=32 << 20),
        name="correct",
    )(
        place, tau, adjacency, toa, up, down, left, right,
        from_left, from_left, from_right, from_right, row_mat, col_mat,
        cells, up, down, left, right, from_left, from_left, from_right, from_right,
    )


def body(toa, aot_seed, valid, cloud, land_class, row_taps, col_taps, tau, adjacency):
    cell_rows, cell_cols = aot_seed.shape
    grid_rows = cell_rows * lax.axis_size("along")
    grid_cols = cell_cols * lax.axis_size("across")
    place = jnp.stack(
        [
            lax.axis_index("along") * cell_rows,
            lax.axis_index("across") * cell_cols,
            jnp.int32(grid_rows),
            jnp.int32(grid_cols),
        ]
    ).astype(jnp.int32)
    high = lax.reduce_precision(aot_seed, 8, 7)
    rest = aot_seed - high
    middle = lax.reduce_precision(rest, 8, 7)
    low = rest - middle
    conf = (valid * (1 - cloud)).astype(F32)
    values = jnp.stack([high, middle, low, conf, land_class.astype(F32), jnp.zeros_like(high)])
    values = values.astype(BF16)
    wide = jnp.concatenate([values[:, :, 4:8], values, values[:, :, 0:4]], axis=2)
    cells = jnp.pad(wide, ((0, 0), (6, 4), (0, 112)))
    twice = jnp.pad(wide, ((0, 0), (0, 0), (0, 112)))
    twice = jnp.concatenate([twice, twice], axis=2)
    row_at = iota((BANDS, HALO, COLS), 1)
    go_down = jnp.where(
        row_at < HALO - KR,
        jnp.pad(twice[:, 2:6], ((0, 0), (0, KR), (0, 0))),
        toa[:, ROWS - HALO :, :],
    )
    go_up = jnp.where(
        row_at < KR,
        toa[:, :HALO, :],
        jnp.pad(twice[:, 0:4], ((0, 0), (KR, 0), (0, 0))),
    )
    up = shift(go_down, "along", 1)
    down = shift(go_up, "along", -1)
    lane_at = iota((BANDS, ROWS, SIDE), 2)
    go_right = jnp.where(
        lane_at < SIDE - KR,
        jnp.pad(wide, ((0, 0), (6, ROWS - 12), (0, 112))),
        toa[:, :, COLS - SIDE :],
    )
    go_left = jnp.where(
        lane_at < KR,
        toa[:, :, :SIDE],
        jnp.pad(wide, ((0, 0), (6, ROWS - 12), (112, 0))),
    )
    left = shift(go_right, "across", 1)
    right = shift(go_left, "across", -1)
    row_mat, col_mat = toeplitz(row_taps, col_taps)
    both = jnp.concatenate([up, down], axis=0)
    from_left = shift(both[:, :, COLS - SIDE :], "across", 1)
    from_right = shift(both[:, :, :SIDE], "across", -1)
    return correct(
        place, tau, adjacency, toa, up, down, left, right, from_left, from_right,
        row_mat, col_mat, cells,
    )


def solution(mesh):
    cells = P("along", "across")
    in_specs = (P(None, "along", "across"), cells, cells, cells, cells, P(), P(), P(), P())
    out_specs = P(None, "along", "across")
    return jax.shard_map(body, mesh=mesh, in_specs=in_specs, out_specs=out_specs, check_vma=False)
```

```python
import jax
import jax.numpy as jnp
from jax import lax
from jax.experimental import pallas as pl
from jax.experimental.pallas import tpu as pltpu
from jax.sharding import PartitionSpec as P

BANDS = 6
KR = 100
TAPS = 201
CB = 32
SWEEPS = 4
ROWS = 192
COLS = 256
HALO = 104
SIDE = 128
CELL_ROWS = 6
CELL_COLS = 8
UNROLL_OWN = False
UNROLL_LAST = True
F32 = jnp.float32
BF16 = jnp.bfloat16
VMEM = pl.BlockSpec(memory_space=pltpu.VMEM)
SMEM = pl.BlockSpec(memory_space=pltpu.SMEM)


def iota(shape, dim):
    return lax.broadcasted_iota(jnp.int32, shape, dim)


def shift(value, axis, step):
    count = lax.axis_size(axis)
    pairs = [(i, i + step) for i in range(count) if 0 <= i + step < count]
    return lax.ppermute(value, axis, pairs)


def swap(value, first):
    count = lax.axis_size("across")
    pairs = []
    for i in range(first, count - 1, 2):
        pairs += [(i, i + 1), (i + 1, i)]
    return lax.ppermute(value, "across", pairs)


def vmem_out(*shapes):
    return [pltpu.VMEM(shape, dtype) for shape, dtype in shapes]


def pack_kernel(
    toa_in, seed_in, valid_in, cloud_in, land_in, row_in, col_in,
    go_down, go_up, outer, inner, cells, toa, row_taps, col_taps,
    seed, valid, cloud, land, spot, sems,
):
    moves = [
        (seed_in, seed),
        (valid_in, valid),
        (cloud_in, cloud),
        (land_in, land),
        (toa_in, toa),
        (row_in, row_taps),
        (col_in, col_taps),
    ]
    copies = [pltpu.make_async_copy(x, y, sems.at[i]) for i, (x, y) in enumerate(moves)]
    for copy in copies:
        copy.start()
    for copy in copies[:4]:
        copy.wait()
    core = lax.rem(lax.axis_index("across"), 2)
    sub = iota((8, 128), 0)
    lane = iota((8, 128), 1)
    lane_at = iota((16, 128), 1)
    row_at = iota((16, 128), 0)
    whole = seed[...]
    high = whole.astype(BF16).astype(F32)
    rest = whole - high
    middle = rest.astype(BF16).astype(F32)
    conf = (valid[...] * (1 - cloud[...])).astype(F32)
    values = [high, middle, rest - middle, conf, land[...].astype(F32)]
    copies[4].wait()
    go_down[...] = toa[:, ROWS - HALO :, :]
    go_up[...] = toa[:, :HALO, :]

    def side(ref, offset):
        ref[...] = toa[:, :, offset : offset + SIDE]

    @pl.when(core == 0)
    def _():
        side(outer, 0)
        side(inner, SIDE)

    @pl.when(core == 1)
    def _():
        side(outer, SIDE)
        side(inner, 0)

    spot[...] = jnp.zeros_like(spot)
    blank = jnp.zeros((8, 128), F32)
    for v in range(5):
        spot[0:CELL_ROWS, 4 : 4 + CELL_COLS] = values[v]
        base = spot[...]
        wide = jnp.where(
            lane < 4,
            pltpu.roll(base, 120, 1),
            jnp.where(lane < 12, base, jnp.where(lane < 16, pltpu.roll(base, 8, 1), 0.0)),
        )
        turned = pltpu.roll(wide, 6, 0)
        head = jnp.where(sub < 4, turned, 0.0)
        tile = jnp.concatenate([jnp.where(sub >= 6, turned, 0.0), head], axis=0)
        cells[v] = tile
        first = jnp.concatenate([head, blank], axis=0).astype(BF16)
        last = jnp.concatenate([blank, pltpu.roll(wide, 4, 0)], axis=0).astype(BF16)
        for at in (0, 128):
            go_down[v, 0:16, at : at + 128] = jnp.where(
                row_at < HALO - KR, first, toa[v, ROWS - HALO : ROWS - HALO + 16, at : at + 128]
            )
            go_up[v, HALO - 16 : HALO, at : at + 128] = jnp.where(
                row_at >= 16 - (HALO - KR), last, toa[v, HALO - 16 : HALO, at : at + 128]
            )
        to_right = jnp.where(lane_at < SIDE - KR, tile.astype(BF16), toa[v, 0:16, SIDE:])
        to_left = jnp.where(
            lane_at < KR, toa[v, 0:16, 0:SIDE], pltpu.roll(tile, 112, 1).astype(BF16)
        )
        outer[v, 0:16, :] = jnp.where(core == 0, to_left, to_right)
        inner[v, 0:16, :] = jnp.where(core == 0, to_right, to_left)
    copies[5].wait()
    copies[6].wait()


def pack(toa, seed, valid, cloud, land, row_taps, col_taps):
    cell = (CELL_ROWS, CELL_COLS)
    return pl.pallas_call(
        pack_kernel,
        in_specs=[pl.BlockSpec(memory_space=pltpu.HBM)] * 7,
        out_specs=[VMEM] * 8,
        out_shape=vmem_out(
            ((BANDS, HALO, COLS), BF16),
            ((BANDS, HALO, COLS), BF16),
            ((BANDS, ROWS, SIDE), BF16),
            ((BANDS, ROWS, SIDE), BF16),
            ((5, 16, 128), F32),
            ((BANDS, ROWS, COLS), BF16),
            ((BANDS, 3, TAPS), F32),
            ((BANDS, 3, TAPS), F32),
        ),
        scratch_shapes=[
            pltpu.VMEM(cell, F32),
            pltpu.VMEM(cell, jnp.int32),
            pltpu.VMEM(cell, jnp.int32),
            pltpu.VMEM(cell, jnp.int32),
            pltpu.VMEM((8, 128), F32),
            pltpu.SemaphoreType.DMA((7,)),
        ],
        compiler_params=pltpu.CompilerParams(vmem_limit_bytes=58 << 20),
        name="pack",
    )(toa, seed, valid, cloud, land, row_taps, col_taps)


def toeplitz_kernel(row_ref, col_ref, near_out, far_out, col_out, pad_ref):
    pad_ref[...] = jnp.zeros_like(pad_ref)
    flip = (iota((256, 256), 0) + iota((256, 256), 1) == TAPS + 7).astype(F32).astype(BF16)
    col_index = iota((384, 128), 1) - iota((384, 128), 0) + (SIDE + KR)
    col_good = (col_index >= 0) & (col_index < TAPS)
    row_at = iota((ROWS, 256), 1)
    row_base = row_at - iota((ROWS, 256), 0)
    near = row_base + KR
    near_good = (near >= 0) & (near < TAPS) & (row_at < ROWS)
    down_good = row_base + (ROWS + KR) < TAPS
    above = row_base - (2 * HALO - KR)
    above_good = (above >= 0) & (above < TAPS) & (row_at < 2 * HALO)

    def spread(vector, first):
        wide = jnp.broadcast_to(vector, (128, 256))
        return pltpu.roll(wide, first, 1, stride=1, stride_axis=0)

    def tall(value):
        swapped = jnp.concatenate([value[0:64, 128:256], value[0:64, 0:128]], axis=1)
        return jnp.concatenate([value, swapped], axis=0)

    def one(band, carry):
        raw = row_ref[band]
        pad_ref[0:3, 4 : 4 + TAPS] = raw / jnp.sum(raw, axis=-1, keepdims=True)
        raw = col_ref[band]
        pad_ref[8:11, 4 : 4 + TAPS] = raw / jnp.sum(raw, axis=-1, keepdims=True)
        taps = pad_ref[...].astype(BF16)
        flipped = jnp.dot(taps, flip, preferred_element_type=F32)
        taps = taps.astype(F32)
        for kern in range(3):
            rolled = spread(flipped[8 + kern : 9 + kern], 24)
            rolled = jnp.concatenate(
                [rolled[:, 0:128], rolled[:, 128:256], rolled[:, 0:128]], axis=0
            )
            tile = jnp.where(col_good, rolled, 0.0).astype(BF16)
            col_out[band, :, kern * 128 : (kern + 1) * 128] = tile
            vector = taps[kern : kern + 1]
            part = slice(kern * ROWS, (kern + 1) * ROWS)
            near_out[band, part, :] = jnp.where(
                near_good, tall(spread(vector, 152)), 0.0
            ).astype(BF16)
            far_out[band, part, :] = jnp.where(
                down_good,
                tall(spread(vector, 216)),
                jnp.where(above_good, tall(spread(vector, HALO)), 0.0),
            ).astype(BF16)
        return carry

    lax.fori_loop(0, BANDS, one, 0)


def toeplitz(row_taps, col_taps):
    return pl.pallas_call(
        toeplitz_kernel,
        in_specs=[VMEM] * 2,
        out_specs=[VMEM] * 3,
        out_shape=vmem_out(
            ((BANDS, 3 * ROWS, 256), BF16),
            ((BANDS, 3 * ROWS, 256), BF16),
            ((BANDS, 384, 384), BF16),
        ),
        scratch_shapes=[pltpu.VMEM((16, 256), F32)],
        cost_estimate=pl.CostEstimate(flops=0, bytes_accessed=8_000_000, transcendentals=0),
        compiler_params=pltpu.CompilerParams(vmem_limit_bytes=8 << 20),
        name="toeplitz",
    )(row_taps, col_taps)


def split_kernel(toa, up, down, pace, outer, inner, field):
    del pace
    core = lax.rem(lax.axis_index("across"), 2)

    def fill(left, right):
        left[:, 0:HALO] = down[:, :, 0:SIDE]
        left[:, HALO:] = up[:, :, 0:SIDE]
        right[:, 0:HALO] = down[:, :, SIDE:]
        right[:, HALO:] = up[:, :, SIDE:]

    @pl.when(core == 0)
    def _():
        fill(outer, inner)

    @pl.when(core == 1)
    def _():
        fill(inner, outer)

    field[:, 0:ROWS] = toa[...]
    field[:, ROWS : ROWS + HALO] = down[...]
    field[:, ROWS + HALO :] = up[...]


def split(toa, up, down, pace):
    shape = ((BANDS, 2 * HALO, SIDE), BF16)
    return pl.pallas_call(
        split_kernel,
        in_specs=[VMEM] * 4,
        out_specs=[VMEM] * 3,
        out_shape=vmem_out(shape, shape, ((BANDS, ROWS + 2 * HALO, COLS), BF16)),
        compiler_params=pltpu.CompilerParams(vmem_limit_bytes=4 << 20),
        name="split",
    )(toa, up, down, pace)


def middle_matrix(col_mat, band, kern):
    at = slice(kern * 128, (kern + 1) * 128)
    return jnp.concatenate([col_mat[band, 128:384, at], col_mat[band, 0:256, at]], axis=1)


def side_matrix(col_mat, band, kern):
    at = slice(kern * 128, (kern + 1) * 128)
    blank = jnp.zeros((128, 128), BF16)
    return jnp.concatenate(
        [
            jnp.concatenate([col_mat[band, 0:128, at], blank], axis=1),
            jnp.concatenate([blank, col_mat[band, 256:384, at]], axis=1),
        ],
        axis=0,
    )


def own_kernel(field, outer, inner, near_mat, col_mat, env, halo, passed):
    core = lax.rem(lax.axis_index("across"), 2)
    passed[ROWS:256, :] = jnp.zeros((256 - ROWS, 3 * COLS), BF16)

    def one(band, carry):
        first = outer[band]
        second = inner[band]
        sides = jnp.concatenate(
            [jnp.where(core == 0, first, second), jnp.where(core == 0, second, first)], axis=1
        )
        for kern in range(3):
            at = slice(kern * COLS, (kern + 1) * COLS)
            middle = middle_matrix(col_mat, band, kern)
            value = jnp.dot(field[band], middle, preferred_element_type=F32)
            halo[band, :, at] = value[ROWS:]
            value = value[0:ROWS] + jnp.dot(
                sides, side_matrix(col_mat, band, kern), preferred_element_type=F32
            )
            passed[0:ROWS, at] = value.astype(BF16)
        for kern in range(3):
            at = slice(kern * COLS, (kern + 1) * COLS)
            env[band, :, at] = jnp.dot(
                near_mat[band, kern * ROWS : (kern + 1) * ROWS, :],
                passed[:, at],
                preferred_element_type=F32,
            )
        return carry

    lax.fori_loop(0, BANDS, one, 0, unroll=UNROLL_OWN)


def own_part(field, outer, inner, near_mat, col_mat):
    flops = BANDS * 2 * (192 * 512 * 768 + 208 * 256 * 768 + 192 * 256 * 768)
    return pl.pallas_call(
        own_kernel,
        in_specs=[VMEM] * 5,
        out_specs=[VMEM] * 2,
        out_shape=vmem_out(
            ((BANDS, ROWS, 3 * COLS), F32), ((BANDS, 2 * HALO, 3 * COLS), F32)
        ),
        scratch_shapes=[pltpu.VMEM((256, 3 * COLS), BF16)],
        cost_estimate=pl.CostEstimate(
            flops=flops, bytes_accessed=10_000_000, transcendentals=0
        ),
        compiler_params=pltpu.CompilerParams(vmem_limit_bytes=8 << 20),
        name="own_part",
    )(field, outer, inner, near_mat, col_mat)


def cell_state(core, cells, up, down, outer, inner, far_outer, far_inner):
    sub = iota((8, 128), 0)
    lane = iota((8, 128), 1)
    both = iota((16, 128), 1)
    parts = []
    for v in range(5):
        out_up = far_outer[v, HALO : HALO + 8, :].astype(F32)
        in_up = far_inner[v, HALO : HALO + 8, :].astype(F32)
        out_down = far_outer[v, HALO - 8 : HALO, :].astype(F32)
        in_down = far_inner[v, HALO - 8 : HALO, :].astype(F32)
        out_side = outer[v, 0:16, :].astype(F32)
        in_side = inner[v, 0:16, :].astype(F32)
        top = jnp.where(
            lane < 4,
            jnp.where(core == 0, out_up, in_up),
            jnp.where(lane < 12, up[v, 0:8, 0:128].astype(F32), jnp.where(core == 0, in_up, out_up)),
        )
        low = jnp.where(
            lane < 4,
            jnp.where(core == 0, out_down, in_down),
            jnp.where(
                lane < 12,
                down[v, HALO - 8 : HALO, 0:128].astype(F32),
                jnp.where(core == 0, in_down, out_down),
            ),
        )
        west = jnp.where(core == 0, out_side, in_side)
        east = pltpu.roll(jnp.where(core == 0, in_side, out_side), 16, 1)
        middle = jnp.where(both < 4, west, jnp.where(both < 12, cells[v], east))
        first = jnp.where(sub < 6, pltpu.roll(top, 2, 0), middle[0:8])
        second = jnp.where(sub < 4, middle[8:16], low)
        parts.append(jnp.concatenate([first, second], axis=0))
    seed = parts[0] + parts[1] + parts[2]
    conf = parts[3]
    kind = parts[4]
    prior = jnp.where(kind < 0.5, 0.06, jnp.where(kind < 1.5, 0.2, 0.45))
    row = lax.axis_index("along") * CELL_ROWS + iota((16, 128), 0) - 6
    col = lax.axis_index("across") * CELL_COLS + iota((16, 128), 1) - 4
    last_row = lax.axis_size("along") * CELL_ROWS - 1
    last_col = lax.axis_size("across") * CELL_COLS - 1
    inside = (row >= 0) & (row <= last_row) & (col >= 0) & (col <= last_col)
    count = (
        (row > 0).astype(F32)
        + (row < last_row).astype(F32)
        + (col > 0).astype(F32)
        + (col < last_col).astype(F32)
    )
    count = jnp.maximum(count, 1.0)
    fix = conf * seed + (1.0 - conf) * (0.3 * prior)
    mult = 0.7 * (1.0 - conf)
    aot = jnp.where(inside, conf * seed + (1.0 - conf) * prior, 0.0)
    for _ in range(SWEEPS):
        near = (
            pltpu.roll(aot, 15, 0)
            + pltpu.roll(aot, 1, 0)
            + pltpu.roll(aot, 127, 1)
            + pltpu.roll(aot, 1, 1)
        )
        aot = jnp.where(inside, fix + mult * (near / count), 0.0)
    return pltpu.roll(aot, 10, 0)[0:8]


def last_kernel(
    tau, adjacency, toa, up, down, outer, inner, cells, far_outer, far_inner,
    far_mat, col_mat, env, halo, out, passed, fine, result, sems,
):
    core = lax.rem(lax.axis_index("across"), 2)
    small = cell_state(core, cells, up, down, outer, inner, far_outer, far_inner)
    block = iota((8, COLS), 1) // CB
    aot = jnp.zeros((8, COLS), F32)
    for j in range(CELL_COLS):
        aot = jnp.where(block == j, small[:, 4 + j : 5 + j], aot)
    gauss = []
    for center in (0.1, 0.35, 0.7):
        offset = aot - center
        gauss.append(jnp.exp(-(offset * offset) / 0.08))
    total = gauss[0] + gauss[1] + gauss[2]
    fine[0:8, :] = aot
    for kern in range(3):
        fine[8 + 8 * kern : 16 + 8 * kern, :] = gauss[kern] / total
    passed[2 * HALO : 256, :] = jnp.zeros((256 - 2 * HALO, 3 * COLS), BF16)

    def copy(band):
        return pltpu.make_async_copy(result.at[band], out.at[band], sems.at[band])

    def one(band, carry):
        first = far_outer[band]
        second = far_inner[band]
        sides = jnp.concatenate(
            [jnp.where(core == 0, first, second), jnp.where(core == 0, second, first)], axis=1
        )
        for kern in range(3):
            at = slice(kern * COLS, (kern + 1) * COLS)
            value = jnp.dot(
                sides, side_matrix(col_mat, band, kern), preferred_element_type=F32
            )
            passed[0 : 2 * HALO, at] = (value + halo[band, :, at]).astype(BF16)
        growth = jnp.exp(tau[band] * fine[0:8, :])
        own = (1.0 + adjacency[band]) * growth
        scaled = adjacency[band] * growth
        sums = [
            env[band, :, kern * COLS : (kern + 1) * COLS]
            + jnp.dot(
                far_mat[band, kern * ROWS : (kern + 1) * ROWS, :],
                passed[:, kern * COLS : (kern + 1) * COLS],
                preferred_element_type=F32,
            )
            for kern in range(3)
        ]
        weights = [scaled * fine[8 + 8 * kern : 16 + 8 * kern, :] for kern in range(3)]
        for i in range(CELL_ROWS):
            part = slice(i * CB, (i + 1) * CB)
            value = own[i : i + 1, :] * toa[band, part, :].astype(F32)
            for kern in range(3):
                value = value - weights[kern][i : i + 1, :] * sums[kern][part, :]
            result[band, part, :] = value
        copy(band).start()
        return carry

    lax.fori_loop(0, BANDS, one, 0, unroll=UNROLL_LAST)
    for band in range(BANDS):
        copy(band).wait()


def last_part(tau, adjacency, toa, up, down, outer, inner, cells, far_outer, far_inner, far_mat, col_mat, env, halo):
    flops = BANDS * 2 * (208 * 256 * 768 + 192 * 256 * 768)
    return pl.pallas_call(
        last_kernel,
        in_specs=[SMEM, SMEM] + [VMEM] * 12,
        out_specs=pl.BlockSpec(memory_space=pl.ANY),
        out_shape=jax.ShapeDtypeStruct((BANDS, ROWS, COLS), F32),
        scratch_shapes=[
            pltpu.VMEM((256, 3 * COLS), BF16),
            pltpu.VMEM((32, COLS), F32),
            pltpu.VMEM((BANDS, ROWS, COLS), F32),
            pltpu.SemaphoreType.DMA((BANDS,)),
        ],
        cost_estimate=pl.CostEstimate(
            flops=flops, bytes_accessed=12_000_000, transcendentals=0
        ),
        compiler_params=pltpu.CompilerParams(vmem_limit_bytes=8 << 20),
        name="last_part",
    )(
        tau, adjacency, toa, up, down, outer, inner, cells, far_outer, far_inner,
        far_mat, col_mat, env, halo,
    )


def body(toa, aot_seed, valid, cloud, land_class, row_taps, col_taps, tau, adjacency):
    go_down, go_up, to_outer, to_inner, cells, toa, row_taps, col_taps = pack(
        toa, aot_seed, valid, cloud, land_class, row_taps, col_taps
    )
    up = shift(go_down, "along", 1)
    down = shift(go_up, "along", -1)
    outer = swap(to_outer, 1)
    inner = swap(to_inner, 0)
    near_mat, far_mat, col_mat = toeplitz(row_taps, col_taps)
    far_to_outer, far_to_inner, field = split(toa, up, down, near_mat)
    far_outer = swap(far_to_outer, 1)
    far_inner = swap(far_to_inner, 0)
    env, halo = own_part(field, outer, inner, near_mat, col_mat)
    return last_part(
        tau, adjacency, toa, up, down, outer, inner, cells, far_outer, far_inner,
        far_mat, col_mat, env, halo,
    )


def solution(mesh):
    cells = P("along", "across")
    in_specs = (P(None, "along", "across"), cells, cells, cells, cells, P(), P(), P(), P())
    out_specs = P(None, "along", "across")
    return jax.shard_map(body, mesh=mesh, in_specs=in_specs, out_specs=out_specs, check_vma=False)
```

```python
import jax
import jax.numpy as jnp
from jax import lax
from jax.experimental import pallas as pl
from jax.experimental.pallas import tpu as pltpu
from jax.sharding import PartitionSpec as P

BANDS = 6
KR = 100
TAPS = 201
CB = 32
SWEEPS = 4
ROWS = 192
COLS = 256
HALO = 104
SIDE = 128
CELL_ROWS = 6
CELL_COLS = 8
F32 = jnp.float32
BF16 = jnp.bfloat16
VMEM = pl.BlockSpec(memory_space=pltpu.VMEM)
SMEM = pl.BlockSpec(memory_space=pltpu.SMEM)


def iota(shape, dim):
    return lax.broadcasted_iota(jnp.int32, shape, dim)


def exchange(value, step):
    rows = lax.axis_size("along")
    cols = lax.axis_size("across")
    pairs = []
    for i in range(rows):
        for j in range(cols):
            to = i + (step if j % 2 == 0 else -step)
            if 0 <= to < rows:
                pairs.append((i * cols + j, to * cols + j))
    return lax.ppermute(value, ("along", "across"), pairs)


def swap(value, first):
    count = lax.axis_size("across")
    pairs = []
    for i in range(first, count - 1, 2):
        pairs += [(i, i + 1), (i + 1, i)]
    return lax.ppermute(value, "across", pairs)


def vmem_out(*shapes):
    return [pltpu.VMEM(shape, dtype) for shape, dtype in shapes]


def pack_kernel(
    toa_in, seed_in, valid_in, cloud_in, land_in, row_in, col_in,
    early, late, outer, inner, cells, toa, row_taps, col_taps,
    seed, valid, cloud, land, spot, sems,
):
    moves = [
        (seed_in, seed),
        (valid_in, valid),
        (cloud_in, cloud),
        (land_in, land),
        (toa_in, toa),
        (row_in, row_taps),
        (col_in, col_taps),
    ]
    copies = [pltpu.make_async_copy(x, y, sems.at[i]) for i, (x, y) in enumerate(moves)]
    for copy in copies:
        copy.start()
    for copy in copies[:4]:
        copy.wait()
    core = lax.rem(lax.axis_index("across"), 2)
    sub = iota((8, 128), 0)
    lane = iota((8, 128), 1)
    lane_at = iota((16, 128), 1)
    row_at = iota((16, 128), 0)
    whole = seed[...]
    high = whole.astype(BF16).astype(F32)
    rest = whole - high
    middle = rest.astype(BF16).astype(F32)
    conf = (valid[...] * (1 - cloud[...])).astype(F32)
    values = [high, middle, rest - middle, conf, land[...].astype(F32)]
    blank = jnp.zeros((8, 128), F32)
    spot[...] = jnp.zeros_like(spot)
    tiles = []
    for v in range(5):
        spot[0:CELL_ROWS, 4 : 4 + CELL_COLS] = values[v]
        base = spot[...]
        wide = jnp.where(
            lane < 4,
            pltpu.roll(base, 120, 1),
            jnp.where(lane < 12, base, jnp.where(lane < 16, pltpu.roll(base, 8, 1), 0.0)),
        )
        turned = pltpu.roll(wide, 6, 0)
        head = jnp.where(sub < 4, turned, 0.0)
        tile = jnp.concatenate([jnp.where(sub >= 6, turned, 0.0), head], axis=0)
        cells[v] = tile
        tiles.append(
            (
                jnp.concatenate([head, blank], axis=0).astype(BF16),
                jnp.concatenate([blank, pltpu.roll(wide, 4, 0)], axis=0).astype(BF16),
                tile.astype(BF16),
                pltpu.roll(tile, 112, 1).astype(BF16),
            )
        )
    copies[4].wait()

    def fill(go_down, go_up, to_left, to_right):
        go_down[...] = toa[:, ROWS - HALO :, :]
        go_up[...] = toa[:, :HALO, :]
        to_left[...] = toa[:, :, :SIDE]
        to_right[...] = toa[:, :, SIDE:]
        for v in range(5):
            first, last, left_cells, right_cells = tiles[v]
            for at in (0, 128):
                go_down[v, 0:16, at : at + 128] = jnp.where(
                    row_at < HALO - KR,
                    first,
                    toa[v, ROWS - HALO : ROWS - HALO + 16, at : at + 128],
                )
                go_up[v, HALO - 16 : HALO, at : at + 128] = jnp.where(
                    row_at >= 16 - (HALO - KR), last, toa[v, HALO - 16 : HALO, at : at + 128]
                )
            to_right[v, 0:16, :] = jnp.where(
                lane_at < SIDE - KR, left_cells, toa[v, 0:16, SIDE:]
            )
            to_left[v, 0:16, :] = jnp.where(lane_at < KR, toa[v, 0:16, 0:SIDE], right_cells)

    @pl.when(core == 0)
    def _():
        fill(early, late, outer, inner)

    @pl.when(core == 1)
    def _():
        fill(late, early, inner, outer)

    copies[5].wait()
    copies[6].wait()


def pack(toa, seed, valid, cloud, land, row_taps, col_taps):
    cell = (CELL_ROWS, CELL_COLS)
    return pl.pallas_call(
        pack_kernel,
        in_specs=[pl.BlockSpec(memory_space=pltpu.HBM)] * 7,
        out_specs=[VMEM] * 8,
        out_shape=vmem_out(
            ((BANDS, HALO, COLS), BF16),
            ((BANDS, HALO, COLS), BF16),
            ((BANDS, ROWS, SIDE), BF16),
            ((BANDS, ROWS, SIDE), BF16),
            ((5, 16, 128), F32),
            ((BANDS, ROWS, COLS), BF16),
            ((BANDS, 3, TAPS), F32),
            ((BANDS, 3, TAPS), F32),
        ),
        scratch_shapes=[
            pltpu.VMEM(cell, F32),
            pltpu.VMEM(cell, jnp.int32),
            pltpu.VMEM(cell, jnp.int32),
            pltpu.VMEM(cell, jnp.int32),
            pltpu.VMEM((8, 128), F32),
            pltpu.SemaphoreType.DMA((7,)),
        ],
        compiler_params=pltpu.CompilerParams(vmem_limit_bytes=58 << 20),
        name="pack",
    )(toa, seed, valid, cloud, land, row_taps, col_taps)


def toeplitz_kernel(row_ref, col_ref, near_out, far_out, col_out, pad_ref):
    pad_ref[...] = jnp.zeros_like(pad_ref)
    flip = (iota((256, 256), 0) + iota((256, 256), 1) == TAPS + 7).astype(F32).astype(BF16)
    col_index = iota((384, 128), 1) - iota((384, 128), 0) + (SIDE + KR)
    col_good = (col_index >= 0) & (col_index < TAPS)
    row_at = iota((ROWS, 256), 1)
    row_base = row_at - iota((ROWS, 256), 0)
    near = row_base + KR
    near_good = (near >= 0) & (near < TAPS) & (row_at < ROWS)
    down_good = row_base + (ROWS + KR) < TAPS
    above = row_base - (2 * HALO - KR)
    above_good = (above >= 0) & (above < TAPS) & (row_at < 2 * HALO)

    def spread(vector, first):
        wide = jnp.broadcast_to(vector, (128, 256))
        return pltpu.roll(wide, first, 1, stride=1, stride_axis=0)

    def tall(value):
        swapped = jnp.concatenate([value[0:64, 128:256], value[0:64, 0:128]], axis=1)
        return jnp.concatenate([value, swapped], axis=0)

    def one(band, carry):
        raw = row_ref[band]
        pad_ref[0:3, 4 : 4 + TAPS] = raw / jnp.sum(raw, axis=-1, keepdims=True)
        raw = col_ref[band]
        pad_ref[8:11, 4 : 4 + TAPS] = raw / jnp.sum(raw, axis=-1, keepdims=True)
        taps = pad_ref[...].astype(BF16)
        flipped = jnp.dot(taps, flip, preferred_element_type=F32)
        taps = taps.astype(F32)
        for kern in range(3):
            rolled = spread(flipped[8 + kern : 9 + kern], 24)
            rolled = jnp.concatenate(
                [rolled[:, 0:128], rolled[:, 128:256], rolled[:, 0:128]], axis=0
            )
            tile = jnp.where(col_good, rolled, 0.0).astype(BF16)
            col_out[band, :, kern * 128 : (kern + 1) * 128] = tile
            vector = taps[kern : kern + 1]
            part = slice(kern * ROWS, (kern + 1) * ROWS)
            near_out[band, part, :] = jnp.where(
                near_good, tall(spread(vector, 152)), 0.0
            ).astype(BF16)
            far_out[band, part, :] = jnp.where(
                down_good,
                tall(spread(vector, 216)),
                jnp.where(above_good, tall(spread(vector, HALO)), 0.0),
            ).astype(BF16)
        return carry

    lax.fori_loop(0, BANDS, one, 0, unroll=True)


def toeplitz(row_taps, col_taps):
    return pl.pallas_call(
        toeplitz_kernel,
        in_specs=[VMEM] * 2,
        out_specs=[VMEM] * 3,
        out_shape=vmem_out(
            ((BANDS, 3 * ROWS, 256), BF16),
            ((BANDS, 3 * ROWS, 256), BF16),
            ((BANDS, 384, 384), BF16),
        ),
        scratch_shapes=[pltpu.VMEM((16, 256), F32)],
        cost_estimate=pl.CostEstimate(flops=0, bytes_accessed=8_000_000, transcendentals=0),
        compiler_params=pltpu.CompilerParams(vmem_limit_bytes=8 << 20),
        name="toeplitz",
    )(row_taps, col_taps)


def split_kernel(toa, early, late, pace, outer, inner, field):
    del pace
    core = lax.rem(lax.axis_index("across"), 2)

    def fill(up, down, left, right):
        left[:, 0:HALO] = down[:, :, 0:SIDE]
        left[:, HALO:] = up[:, :, 0:SIDE]
        right[:, 0:HALO] = down[:, :, SIDE:]
        right[:, HALO:] = up[:, :, SIDE:]
        field[:, ROWS : ROWS + HALO] = down[...]
        field[:, ROWS + HALO :] = up[...]

    @pl.when(core == 0)
    def _():
        fill(early, late, outer, inner)

    @pl.when(core == 1)
    def _():
        fill(late, early, inner, outer)

    field[:, 0:ROWS] = toa[...]


def split(toa, early, late, pace):
    shape = ((BANDS, 2 * HALO, SIDE), BF16)
    return pl.pallas_call(
        split_kernel,
        in_specs=[VMEM] * 4,
        out_specs=[VMEM] * 3,
        out_shape=vmem_out(shape, shape, ((BANDS, ROWS + 2 * HALO, COLS), BF16)),
        compiler_params=pltpu.CompilerParams(vmem_limit_bytes=4 << 20),
        name="split",
    )(toa, early, late, pace)


def middle_matrix(col_mat, band, kern):
    at = slice(kern * 128, (kern + 1) * 128)
    return jnp.concatenate([col_mat[band, 128:384, at], col_mat[band, 0:256, at]], axis=1)


def side_matrix(col_mat, band, kern):
    at = slice(kern * 128, (kern + 1) * 128)
    blank = jnp.zeros((128, 128), BF16)
    return jnp.concatenate(
        [
            jnp.concatenate([col_mat[band, 0:128, at], blank], axis=1),
            jnp.concatenate([blank, col_mat[band, 256:384, at]], axis=1),
        ],
        axis=0,
    )


def own_kernel(field, outer, inner, near_mat, col_mat, env, halo, passed):
    core = lax.rem(lax.axis_index("across"), 2)
    passed[ROWS:256, :] = jnp.zeros((256 - ROWS, 3 * COLS), BF16)

    def one(band, carry):
        first = outer[band]
        second = inner[band]
        sides = jnp.concatenate(
            [jnp.where(core == 0, first, second), jnp.where(core == 0, second, first)], axis=1
        )
        for kern in range(3):
            at = slice(kern * COLS, (kern + 1) * COLS)
            middle = middle_matrix(col_mat, band, kern)
            value = jnp.dot(field[band], middle, preferred_element_type=F32)
            halo[band, :, at] = value[ROWS:]
            value = value[0:ROWS] + jnp.dot(
                sides, side_matrix(col_mat, band, kern), preferred_element_type=F32
            )
            passed[0:ROWS, at] = value.astype(BF16)
        for kern in range(3):
            at = slice(kern * COLS, (kern + 1) * COLS)
            env[band, :, at] = jnp.dot(
                near_mat[band, kern * ROWS : (kern + 1) * ROWS, :],
                passed[:, at],
                preferred_element_type=F32,
            )
        return carry

    lax.fori_loop(0, BANDS, one, 0, unroll=True)


def own_part(field, outer, inner, near_mat, col_mat):
    flops = BANDS * 2 * (192 * 512 * 768 + 208 * 256 * 768 + 192 * 256 * 768)
    return pl.pallas_call(
        own_kernel,
        in_specs=[VMEM] * 5,
        out_specs=[VMEM] * 2,
        out_shape=vmem_out(
            ((BANDS, ROWS, 3 * COLS), F32), ((BANDS, 2 * HALO, 3 * COLS), F32)
        ),
        scratch_shapes=[pltpu.VMEM((256, 3 * COLS), BF16)],
        cost_estimate=pl.CostEstimate(
            flops=flops, bytes_accessed=10_000_000, transcendentals=0
        ),
        compiler_params=pltpu.CompilerParams(vmem_limit_bytes=8 << 20),
        name="own_part",
    )(field, outer, inner, near_mat, col_mat)


def cell_state(core, cells, field, outer, inner, far_outer, far_inner):
    low_at = ROWS + HALO
    sub = iota((8, 128), 0)
    lane = iota((8, 128), 1)
    both = iota((16, 128), 1)
    parts = []
    for v in range(5):
        out_up = far_outer[v, HALO : HALO + 8, :].astype(F32)
        in_up = far_inner[v, HALO : HALO + 8, :].astype(F32)
        out_down = far_outer[v, HALO - 8 : HALO, :].astype(F32)
        in_down = far_inner[v, HALO - 8 : HALO, :].astype(F32)
        out_side = outer[v, 0:16, :].astype(F32)
        in_side = inner[v, 0:16, :].astype(F32)
        top = jnp.where(
            lane < 4,
            jnp.where(core == 0, out_up, in_up),
            jnp.where(lane < 12, field[v, low_at : low_at + 8, 0:128].astype(F32), jnp.where(core == 0, in_up, out_up)),
        )
        low = jnp.where(
            lane < 4,
            jnp.where(core == 0, out_down, in_down),
            jnp.where(
                lane < 12,
                field[v, low_at - 8 : low_at, 0:128].astype(F32),
                jnp.where(core == 0, in_down, out_down),
            ),
        )
        west = jnp.where(core == 0, out_side, in_side)
        east = pltpu.roll(jnp.where(core == 0, in_side, out_side), 16, 1)
        middle = jnp.where(both < 4, west, jnp.where(both < 12, cells[v], east))
        first = jnp.where(sub < 6, pltpu.roll(top, 2, 0), middle[0:8])
        second = jnp.where(sub < 4, middle[8:16], low)
        parts.append(jnp.concatenate([first, second], axis=0))
    seed = parts[0] + parts[1] + parts[2]
    conf = parts[3]
    kind = parts[4]
    prior = jnp.where(kind < 0.5, 0.06, jnp.where(kind < 1.5, 0.2, 0.45))
    row = lax.axis_index("along") * CELL_ROWS + iota((16, 128), 0) - 6
    col = lax.axis_index("across") * CELL_COLS + iota((16, 128), 1) - 4
    last_row = lax.axis_size("along") * CELL_ROWS - 1
    last_col = lax.axis_size("across") * CELL_COLS - 1
    inside = (row >= 0) & (row <= last_row) & (col >= 0) & (col <= last_col)
    count = (
        (row > 0).astype(F32)
        + (row < last_row).astype(F32)
        + (col > 0).astype(F32)
        + (col < last_col).astype(F32)
    )
    count = jnp.maximum(count, 1.0)
    fix = conf * seed + (1.0 - conf) * (0.3 * prior)
    mult = 0.7 * (1.0 - conf)
    aot = jnp.where(inside, conf * seed + (1.0 - conf) * prior, 0.0)
    for _ in range(SWEEPS):
        near = (
            pltpu.roll(aot, 15, 0)
            + pltpu.roll(aot, 1, 0)
            + pltpu.roll(aot, 127, 1)
            + pltpu.roll(aot, 1, 1)
        )
        aot = jnp.where(inside, fix + mult * (near / count), 0.0)
    return pltpu.roll(aot, 10, 0)[0:8]


def last_kernel(
    tau, adjacency, field, outer, inner, cells, far_outer, far_inner,
    far_mat, col_mat, env, halo, out, passed, fine, result, sems,
):
    core = lax.rem(lax.axis_index("across"), 2)
    small = cell_state(core, cells, field, outer, inner, far_outer, far_inner)
    block = iota((8, COLS), 1) // CB
    aot = jnp.zeros((8, COLS), F32)
    for j in range(CELL_COLS):
        aot = jnp.where(block == j, small[:, 4 + j : 5 + j], aot)
    gauss = []
    for center in (0.1, 0.35, 0.7):
        offset = aot - center
        gauss.append(jnp.exp(-(offset * offset) / 0.08))
    total = gauss[0] + gauss[1] + gauss[2]
    fine[0:8, :] = aot
    for kern in range(3):
        fine[8 + 8 * kern : 16 + 8 * kern, :] = gauss[kern] / total
    passed[2 * HALO : 256, :] = jnp.zeros((256 - 2 * HALO, 3 * COLS), BF16)

    def copy(band):
        return pltpu.make_async_copy(result.at[band], out.at[band], sems.at[band])

    def one(band, carry):
        first = far_outer[band]
        second = far_inner[band]
        sides = jnp.concatenate(
            [jnp.where(core == 0, first, second), jnp.where(core == 0, second, first)], axis=1
        )
        for kern in range(3):
            at = slice(kern * COLS, (kern + 1) * COLS)
            value = jnp.dot(
                sides, side_matrix(col_mat, band, kern), preferred_element_type=F32
            )
            passed[0 : 2 * HALO, at] = (value + halo[band, :, at]).astype(BF16)
        growth = jnp.exp(tau[band] * fine[0:8, :])
        own = (1.0 + adjacency[band]) * growth
        scaled = adjacency[band] * growth
        sums = [
            env[band, :, kern * COLS : (kern + 1) * COLS]
            + jnp.dot(
                far_mat[band, kern * ROWS : (kern + 1) * ROWS, :],
                passed[:, kern * COLS : (kern + 1) * COLS],
                preferred_element_type=F32,
            )
            for kern in range(3)
        ]
        weights = [scaled * fine[8 + 8 * kern : 16 + 8 * kern, :] for kern in range(3)]
        for i in range(CELL_ROWS):
            part = slice(i * CB, (i + 1) * CB)
            value = own[i : i + 1, :] * field[band, part, :].astype(F32)
            for kern in range(3):
                value = value - weights[kern][i : i + 1, :] * sums[kern][part, :]
            result[band, part, :] = value
        copy(band).start()
        return carry

    lax.fori_loop(0, BANDS, one, 0, unroll=True)
    for band in range(BANDS):
        copy(band).wait()


def last_part(tau, adjacency, field, outer, inner, cells, far_outer, far_inner, far_mat, col_mat, env, halo):
    flops = BANDS * 2 * (208 * 256 * 768 + 192 * 256 * 768)
    return pl.pallas_call(
        last_kernel,
        in_specs=[SMEM, SMEM] + [VMEM] * 10,
        out_specs=pl.BlockSpec(memory_space=pl.ANY),
        out_shape=jax.ShapeDtypeStruct((BANDS, ROWS, COLS), F32),
        scratch_shapes=[
            pltpu.VMEM((256, 3 * COLS), BF16),
            pltpu.VMEM((32, COLS), F32),
            pltpu.VMEM((BANDS, ROWS, COLS), F32),
            pltpu.SemaphoreType.DMA((BANDS,)),
        ],
        cost_estimate=pl.CostEstimate(
            flops=flops, bytes_accessed=12_000_000, transcendentals=0
        ),
        compiler_params=pltpu.CompilerParams(vmem_limit_bytes=8 << 20),
        name="last_part",
    )(
        tau, adjacency, field, outer, inner, cells, far_outer, far_inner,
        far_mat, col_mat, env, halo,
    )


def body(toa, aot_seed, valid, cloud, land_class, row_taps, col_taps, tau, adjacency):
    to_early, to_late, to_outer, to_inner, cells, toa, row_taps, col_taps = pack(
        toa, aot_seed, valid, cloud, land_class, row_taps, col_taps
    )
    early = exchange(to_early, 1)
    late = exchange(to_late, -1)
    outer = swap(to_outer, 1)
    inner = swap(to_inner, 0)
    near_mat, far_mat, col_mat = toeplitz(row_taps, col_taps)
    far_to_outer, far_to_inner, field = split(toa, early, late, near_mat)
    far_outer = swap(far_to_outer, 1)
    far_inner = swap(far_to_inner, 0)
    env, halo = own_part(field, outer, inner, near_mat, col_mat)
    return last_part(
        tau, adjacency, field, outer, inner, cells, far_outer, far_inner,
        far_mat, col_mat, env, halo,
    )


def solution(mesh):
    cells = P("along", "across")
    in_specs = (P(None, "along", "across"), cells, cells, cells, cells, P(), P(), P(), P())
    out_specs = P(None, "along", "across")
    return jax.shard_map(body, mesh=mesh, in_specs=in_specs, out_specs=out_specs, check_vma=False)
```

```python
import jax
import jax.numpy as jnp
from jax import lax
from jax.experimental import pallas as pl
from jax.experimental.pallas import tpu as pltpu
from jax.sharding import PartitionSpec as P

BANDS = 6
KR = 100
TAPS = 201
CB = 32
SWEEPS = 4
ROWS = 192
COLS = 256
HALO = 104
SIDE = 128
CELL_ROWS = 6
CELL_COLS = 8
F32 = jnp.float32
BF16 = jnp.bfloat16
VMEM = pl.BlockSpec(memory_space=pltpu.VMEM)
SMEM = pl.BlockSpec(memory_space=pltpu.SMEM)


def iota(shape, dim):
    return lax.broadcasted_iota(jnp.int32, shape, dim)


def exchange(value, step):
    rows = lax.axis_size("along")
    cols = lax.axis_size("across")
    pairs = []
    for i in range(rows):
        for j in range(cols):
            to = i + (step if j % 2 == 0 else -step)
            if 0 <= to < rows:
                pairs.append((i * cols + j, to * cols + j))
    return lax.ppermute(value, ("along", "across"), pairs)


def swap(value, first):
    count = lax.axis_size("across")
    pairs = []
    for i in range(first, count - 1, 2):
        pairs += [(i, i + 1), (i + 1, i)]
    return lax.ppermute(value, "across", pairs)


def vmem_out(*shapes):
    return [pltpu.VMEM(shape, dtype) for shape, dtype in shapes]


def pack_kernel(
    toa_in, seed_in, valid_in, cloud_in, land_in, row_in, col_in,
    early, late, outer, inner, cells, toa, row_taps, col_taps,
    seed, valid, cloud, land, spot, sems,
):
    moves = [
        (seed_in, seed),
        (valid_in, valid),
        (cloud_in, cloud),
        (land_in, land),
        (toa_in, toa),
        (row_in, row_taps),
        (col_in, col_taps),
    ]
    copies = [pltpu.make_async_copy(x, y, sems.at[i]) for i, (x, y) in enumerate(moves)]
    for copy in copies:
        copy.start()
    for copy in copies[:4]:
        copy.wait()
    core = lax.rem(lax.axis_index("across"), 2)
    sub = iota((8, 128), 0)
    lane = iota((8, 128), 1)
    lane_at = iota((16, 128), 1)
    row_at = iota((16, 128), 0)
    whole = seed[...]
    high = whole.astype(BF16).astype(F32)
    rest = whole - high
    middle = rest.astype(BF16).astype(F32)
    conf = (valid[...] * (1 - cloud[...])).astype(F32)
    values = [high, middle, rest - middle, conf, land[...].astype(F32)]
    blank = jnp.zeros((8, 128), F32)
    spot[...] = jnp.zeros_like(spot)
    tiles = []
    for v in range(5):
        spot[0:CELL_ROWS, 4 : 4 + CELL_COLS] = values[v]
        base = spot[...]
        wide = jnp.where(
            lane < 4,
            pltpu.roll(base, 120, 1),
            jnp.where(lane < 12, base, jnp.where(lane < 16, pltpu.roll(base, 8, 1), 0.0)),
        )
        turned = pltpu.roll(wide, 6, 0)
        head = jnp.where(sub < 4, turned, 0.0)
        tile = jnp.concatenate([jnp.where(sub >= 6, turned, 0.0), head], axis=0)
        cells[v] = tile
        tiles.append(
            (
                jnp.concatenate([head, blank], axis=0).astype(BF16),
                jnp.concatenate([blank, pltpu.roll(wide, 4, 0)], axis=0).astype(BF16),
                tile.astype(BF16),
                pltpu.roll(tile, 112, 1).astype(BF16),
            )
        )
    copies[4].wait()

    def fill(go_down, go_up, to_left, to_right):
        go_down[...] = toa[:, ROWS - HALO :, :]
        go_up[...] = toa[:, :HALO, :]
        to_left[...] = toa[:, :, :SIDE]
        to_right[...] = toa[:, :, SIDE:]
        for v in range(5):
            first, last, left_cells, right_cells = tiles[v]
            for at in (0, 128):
                go_down[v, 0:16, at : at + 128] = jnp.where(
                    row_at < HALO - KR,
                    first,
                    toa[v, ROWS - HALO : ROWS - HALO + 16, at : at + 128],
                )
                go_up[v, HALO - 16 : HALO, at : at + 128] = jnp.where(
                    row_at >= 16 - (HALO - KR), last, toa[v, HALO - 16 : HALO, at : at + 128]
                )
            to_right[v, 0:16, :] = jnp.where(
                lane_at < SIDE - KR, left_cells, toa[v, 0:16, SIDE:]
            )
            to_left[v, 0:16, :] = jnp.where(lane_at < KR, toa[v, 0:16, 0:SIDE], right_cells)

    @pl.when(core == 0)
    def _():
        fill(early, late, outer, inner)

    @pl.when(core == 1)
    def _():
        fill(late, early, inner, outer)

    copies[5].wait()
    copies[6].wait()


def pack(toa, seed, valid, cloud, land, row_taps, col_taps):
    cell = (CELL_ROWS, CELL_COLS)
    return pl.pallas_call(
        pack_kernel,
        in_specs=[pl.BlockSpec(memory_space=pltpu.HBM)] * 7,
        out_specs=[VMEM] * 8,
        out_shape=vmem_out(
            ((BANDS, HALO, COLS), BF16),
            ((BANDS, HALO, COLS), BF16),
            ((BANDS, ROWS, SIDE), BF16),
            ((BANDS, ROWS, SIDE), BF16),
            ((5, 16, 128), F32),
            ((BANDS, ROWS, COLS), BF16),
            ((BANDS, 3, TAPS), F32),
            ((BANDS, 3, TAPS), F32),
        ),
        scratch_shapes=[
            pltpu.VMEM(cell, F32),
            pltpu.VMEM(cell, jnp.int32),
            pltpu.VMEM(cell, jnp.int32),
            pltpu.VMEM(cell, jnp.int32),
            pltpu.VMEM((8, 128), F32),
            pltpu.SemaphoreType.DMA((7,)),
        ],
        compiler_params=pltpu.CompilerParams(vmem_limit_bytes=58 << 20),
        name="pack",
    )(toa, seed, valid, cloud, land, row_taps, col_taps)


def toeplitz_kernel(row_ref, col_ref, near_out, far_out, col_out, pad_ref):
    pad_ref[...] = jnp.zeros_like(pad_ref)
    for band in range(BANDS):
        pad_ref[8 * band : 8 * band + 3, 4 : 4 + TAPS] = row_ref[band]
        pad_ref[8 * band + 4 : 8 * band + 7, 4 : 4 + TAPS] = col_ref[band]
    raw = pad_ref[...]
    total = jnp.sum(raw, axis=-1, keepdims=True)
    all_taps = (raw / jnp.where(total > 0.0, total, 1.0)).astype(BF16)
    flip = (iota((256, 256), 0) + iota((256, 256), 1) == TAPS + 7).astype(F32).astype(BF16)
    all_flipped = jnp.dot(all_taps, flip, preferred_element_type=F32)
    all_taps = all_taps.astype(F32)
    col_index = iota((384, 128), 1) - iota((384, 128), 0) + (SIDE + KR)
    col_good = (col_index >= 0) & (col_index < TAPS)
    row_at = iota((ROWS, 256), 1)
    row_base = row_at - iota((ROWS, 256), 0)
    near = row_base + KR
    near_good = (near >= 0) & (near < TAPS) & (row_at < ROWS)
    down_good = row_base + (ROWS + KR) < TAPS
    above = row_base - (2 * HALO - KR)
    above_good = (above >= 0) & (above < TAPS) & (row_at < 2 * HALO)

    def spread(vector, first):
        wide = jnp.broadcast_to(vector, (128, 256))
        return pltpu.roll(wide, first, 1, stride=1, stride_axis=0)

    def tall(value):
        swapped = jnp.concatenate([value[0:64, 128:256], value[0:64, 0:128]], axis=1)
        return jnp.concatenate([value, swapped], axis=0)

    for band in range(BANDS):
        for kern in range(3):
            at = 8 * band + 4 + kern
            rolled = spread(all_flipped[at : at + 1], 24)
            rolled = jnp.concatenate(
                [rolled[:, 0:128], rolled[:, 128:256], rolled[:, 0:128]], axis=0
            )
            tile = jnp.where(col_good, rolled, 0.0).astype(BF16)
            col_out[band, :, kern * 128 : (kern + 1) * 128] = tile
            vector = all_taps[8 * band + kern : 8 * band + kern + 1]
            part = slice(kern * ROWS, (kern + 1) * ROWS)
            near_out[band, part, :] = jnp.where(
                near_good, tall(spread(vector, 152)), 0.0
            ).astype(BF16)
            far_out[band, part, :] = jnp.where(
                down_good,
                tall(spread(vector, 216)),
                jnp.where(above_good, tall(spread(vector, HALO)), 0.0),
            ).astype(BF16)


def toeplitz(row_taps, col_taps):
    return pl.pallas_call(
        toeplitz_kernel,
        in_specs=[VMEM] * 2,
        out_specs=[VMEM] * 3,
        out_shape=vmem_out(
            ((BANDS, 3 * ROWS, 256), BF16),
            ((BANDS, 3 * ROWS, 256), BF16),
            ((BANDS, 384, 384), BF16),
        ),
        scratch_shapes=[pltpu.VMEM((8 * BANDS, 256), F32)],
        cost_estimate=pl.CostEstimate(flops=0, bytes_accessed=8_000_000, transcendentals=0),
        compiler_params=pltpu.CompilerParams(vmem_limit_bytes=8 << 20),
        name="toeplitz",
    )(row_taps, col_taps)


def split_kernel(toa, early, late, pace, outer, inner, field):
    del pace
    core = lax.rem(lax.axis_index("across"), 2)

    def fill(up, down, left, right):
        left[:, 0:HALO] = down[:, :, 0:SIDE]
        left[:, HALO:] = up[:, :, 0:SIDE]
        right[:, 0:HALO] = down[:, :, SIDE:]
        right[:, HALO:] = up[:, :, SIDE:]
        field[:, ROWS : ROWS + HALO] = down[...]
        field[:, ROWS + HALO :] = up[...]

    @pl.when(core == 0)
    def _():
        fill(early, late, outer, inner)

    @pl.when(core == 1)
    def _():
        fill(late, early, inner, outer)

    field[:, 0:ROWS] = toa[...]


def split(toa, early, late, pace):
    shape = ((BANDS, 2 * HALO, SIDE), BF16)
    return pl.pallas_call(
        split_kernel,
        in_specs=[VMEM] * 4,
        out_specs=[VMEM] * 3,
        out_shape=vmem_out(shape, shape, ((BANDS, ROWS + 2 * HALO, COLS), BF16)),
        compiler_params=pltpu.CompilerParams(vmem_limit_bytes=4 << 20),
        name="split",
    )(toa, early, late, pace)


def middle_matrix(col_mat, band, kern):
    at = slice(kern * 128, (kern + 1) * 128)
    return jnp.concatenate([col_mat[band, 128:384, at], col_mat[band, 0:256, at]], axis=1)


def side_matrix(col_mat, band, kern):
    at = slice(kern * 128, (kern + 1) * 128)
    blank = jnp.zeros((128, 128), BF16)
    return jnp.concatenate(
        [
            jnp.concatenate([col_mat[band, 0:128, at], blank], axis=1),
            jnp.concatenate([blank, col_mat[band, 256:384, at]], axis=1),
        ],
        axis=0,
    )


def own_kernel(field, outer, inner, near_mat, col_mat, env, halo, passed):
    core = lax.rem(lax.axis_index("across"), 2)
    for slot in range(2):
        passed[slot, ROWS:256, :] = jnp.zeros((256 - ROWS, 3 * COLS), BF16)

    def columns(band):
        first = outer[band]
        second = inner[band]
        sides = jnp.concatenate(
            [jnp.where(core == 0, first, second), jnp.where(core == 0, second, first)], axis=1
        )
        for kern in range(3):
            at = slice(kern * COLS, (kern + 1) * COLS)
            middle = middle_matrix(col_mat, band, kern)
            value = jnp.dot(field[band], middle, preferred_element_type=F32)
            halo[band, :, at] = value[ROWS:]
            value = value[0:ROWS] + jnp.dot(
                sides, side_matrix(col_mat, band, kern), preferred_element_type=F32
            )
            passed[band % 2, 0:ROWS, at] = value.astype(BF16)

    def rows(band):
        for kern in range(3):
            at = slice(kern * COLS, (kern + 1) * COLS)
            env[band, :, at] = jnp.dot(
                near_mat[band, kern * ROWS : (kern + 1) * ROWS, :],
                passed[band % 2, :, at],
                preferred_element_type=F32,
            )

    columns(0)
    for band in range(BANDS):
        if band + 1 < BANDS:
            columns(band + 1)
        rows(band)


def own_part(field, outer, inner, near_mat, col_mat):
    flops = BANDS * 2 * (192 * 512 * 768 + 208 * 256 * 768 + 192 * 256 * 768)
    return pl.pallas_call(
        own_kernel,
        in_specs=[VMEM] * 5,
        out_specs=[VMEM] * 2,
        out_shape=vmem_out(
            ((BANDS, ROWS, 3 * COLS), F32), ((BANDS, 2 * HALO, 3 * COLS), F32)
        ),
        scratch_shapes=[pltpu.VMEM((2, 256, 3 * COLS), BF16)],
        cost_estimate=pl.CostEstimate(
            flops=flops, bytes_accessed=10_000_000, transcendentals=0
        ),
        compiler_params=pltpu.CompilerParams(vmem_limit_bytes=8 << 20),
        name="own_part",
    )(field, outer, inner, near_mat, col_mat)


def cell_state(core, cells, field, outer, inner, far_outer, far_inner):
    low_at = ROWS + HALO
    sub = iota((8, 128), 0)
    lane = iota((8, 128), 1)
    both = iota((16, 128), 1)
    parts = []
    for v in range(5):
        out_up = far_outer[v, HALO : HALO + 8, :].astype(F32)
        in_up = far_inner[v, HALO : HALO + 8, :].astype(F32)
        out_down = far_outer[v, HALO - 8 : HALO, :].astype(F32)
        in_down = far_inner[v, HALO - 8 : HALO, :].astype(F32)
        out_side = outer[v, 0:16, :].astype(F32)
        in_side = inner[v, 0:16, :].astype(F32)
        top = jnp.where(
            lane < 4,
            jnp.where(core == 0, out_up, in_up),
            jnp.where(lane < 12, field[v, low_at : low_at + 8, 0:128].astype(F32), jnp.where(core == 0, in_up, out_up)),
        )
        low = jnp.where(
            lane < 4,
            jnp.where(core == 0, out_down, in_down),
            jnp.where(
                lane < 12,
                field[v, low_at - 8 : low_at, 0:128].astype(F32),
                jnp.where(core == 0, in_down, out_down),
            ),
        )
        west = jnp.where(core == 0, out_side, in_side)
        east = pltpu.roll(jnp.where(core == 0, in_side, out_side), 16, 1)
        middle = jnp.where(both < 4, west, jnp.where(both < 12, cells[v], east))
        first = jnp.where(sub < 6, pltpu.roll(top, 2, 0), middle[0:8])
        second = jnp.where(sub < 4, middle[8:16], low)
        parts.append(jnp.concatenate([first, second], axis=0))
    seed = parts[0] + parts[1] + parts[2]
    conf = parts[3]
    kind = parts[4]
    prior = jnp.where(kind < 0.5, 0.06, jnp.where(kind < 1.5, 0.2, 0.45))
    row = lax.axis_index("along") * CELL_ROWS + iota((16, 128), 0) - 6
    col = lax.axis_index("across") * CELL_COLS + iota((16, 128), 1) - 4
    last_row = lax.axis_size("along") * CELL_ROWS - 1
    last_col = lax.axis_size("across") * CELL_COLS - 1
    inside = (row >= 0) & (row <= last_row) & (col >= 0) & (col <= last_col)
    count = (
        (row > 0).astype(F32)
        + (row < last_row).astype(F32)
        + (col > 0).astype(F32)
        + (col < last_col).astype(F32)
    )
    count = jnp.maximum(count, 1.0)
    fix = conf * seed + (1.0 - conf) * (0.3 * prior)
    mult = 0.7 * (1.0 - conf)
    aot = jnp.where(inside, conf * seed + (1.0 - conf) * prior, 0.0)
    for _ in range(SWEEPS):
        near = (
            pltpu.roll(aot, 15, 0)
            + pltpu.roll(aot, 1, 0)
            + pltpu.roll(aot, 127, 1)
            + pltpu.roll(aot, 1, 1)
        )
        aot = jnp.where(inside, fix + mult * (near / count), 0.0)
    return pltpu.roll(aot, 10, 0)[0:8]


def last_kernel(
    tau, adjacency, field, outer, inner, cells, far_outer, far_inner,
    far_mat, col_mat, env, halo, out, passed, result, sems,
):
    core = lax.rem(lax.axis_index("across"), 2)
    for slot in range(2):
        passed[slot, 2 * HALO : 256, :] = jnp.zeros((256 - 2 * HALO, 3 * COLS), BF16)

    def columns(band):
        first = far_outer[band]
        second = far_inner[band]
        sides = jnp.concatenate(
            [jnp.where(core == 0, first, second), jnp.where(core == 0, second, first)], axis=1
        )
        for kern in range(3):
            at = slice(kern * COLS, (kern + 1) * COLS)
            value = jnp.dot(
                sides, side_matrix(col_mat, band, kern), preferred_element_type=F32
            )
            passed[band % 2, 0 : 2 * HALO, at] = (value + halo[band, :, at]).astype(BF16)

    columns(0)
    small = cell_state(core, cells, field, outer, inner, far_outer, far_inner)
    block = iota((8, COLS), 1) // CB
    aot = jnp.zeros((8, COLS), F32)
    for j in range(CELL_COLS):
        aot = jnp.where(block == j, small[:, 4 + j : 5 + j], aot)
    gauss = []
    for center in (0.1, 0.35, 0.7):
        offset = aot - center
        gauss.append(jnp.exp(-(offset * offset) / 0.08))
    total = gauss[0] + gauss[1] + gauss[2]
    weights = [value / total for value in gauss]

    def copy(band):
        return pltpu.make_async_copy(result.at[band], out.at[band], sems.at[band])

    for band in range(BANDS):
        if band + 1 < BANDS:
            columns(band + 1)
        growth = jnp.exp(tau[band] * aot)
        own = (1.0 + adjacency[band]) * growth
        scaled = adjacency[band] * growth
        factors = [scaled * value for value in weights]
        sums = [
            env[band, :, kern * COLS : (kern + 1) * COLS]
            + jnp.dot(
                far_mat[band, kern * ROWS : (kern + 1) * ROWS, :],
                passed[band % 2, :, kern * COLS : (kern + 1) * COLS],
                preferred_element_type=F32,
            )
            for kern in range(3)
        ]
        for i in range(CELL_ROWS):
            part = slice(i * CB, (i + 1) * CB)
            value = own[i : i + 1, :] * field[band, part, :].astype(F32)
            for kern in range(3):
                value = value - factors[kern][i : i + 1, :] * sums[kern][part, :]
            result[band, part, :] = value
        copy(band).start()
    for band in range(BANDS):
        copy(band).wait()


def last_part(tau, adjacency, field, outer, inner, cells, far_outer, far_inner, far_mat, col_mat, env, halo):
    flops = BANDS * 2 * (208 * 256 * 768 + 192 * 256 * 768)
    return pl.pallas_call(
        last_kernel,
        in_specs=[SMEM, SMEM] + [VMEM] * 10,
        out_specs=pl.BlockSpec(memory_space=pl.ANY),
        out_shape=jax.ShapeDtypeStruct((BANDS, ROWS, COLS), F32),
        scratch_shapes=[
            pltpu.VMEM((2, 256, 3 * COLS), BF16),
            pltpu.VMEM((BANDS, ROWS, COLS), F32),
            pltpu.SemaphoreType.DMA((BANDS,)),
        ],
        cost_estimate=pl.CostEstimate(
            flops=flops, bytes_accessed=12_000_000, transcendentals=0
        ),
        compiler_params=pltpu.CompilerParams(vmem_limit_bytes=8 << 20),
        name="last_part",
    )(
        tau, adjacency, field, outer, inner, cells, far_outer, far_inner,
        far_mat, col_mat, env, halo,
    )


def body(toa, aot_seed, valid, cloud, land_class, row_taps, col_taps, tau, adjacency):
    to_early, to_late, to_outer, to_inner, cells, toa, row_taps, col_taps = pack(
        toa, aot_seed, valid, cloud, land_class, row_taps, col_taps
    )
    early = exchange(to_early, 1)
    late = exchange(to_late, -1)
    outer = swap(to_outer, 1)
    inner = swap(to_inner, 0)
    near_mat, far_mat, col_mat = toeplitz(row_taps, col_taps)
    far_to_outer, far_to_inner, field = split(toa, early, late, near_mat)
    far_outer = swap(far_to_outer, 1)
    far_inner = swap(far_to_inner, 0)
    env, halo = own_part(field, outer, inner, near_mat, col_mat)
    return last_part(
        tau, adjacency, field, outer, inner, cells, far_outer, far_inner,
        far_mat, col_mat, env, halo,
    )


def solution(mesh):
    cells = P("along", "across")
    in_specs = (P(None, "along", "across"), cells, cells, cells, cells, P(), P(), P(), P())
    out_specs = P(None, "along", "across")
    return jax.shard_map(body, mesh=mesh, in_specs=in_specs, out_specs=out_specs, check_vma=False)
```

```python
import jax
import jax.numpy as jnp
from jax import lax
from jax.experimental import pallas as pl
from jax.experimental.pallas import tpu as pltpu
from jax.sharding import PartitionSpec as P

BANDS = 6
KR = 100
TAPS = 201
CB = 32
SWEEPS = 4
ROWS = 192
COLS = 256
HALO = 104
SIDE = 128
CELL_ROWS = 6
CELL_COLS = 8
F32 = jnp.float32
BF16 = jnp.bfloat16
VMEM = pl.BlockSpec(memory_space=pltpu.VMEM)


def iota(shape, dim):
    return lax.broadcasted_iota(jnp.int32, shape, dim)


def exchange(value, step):
    rows = lax.axis_size("along")
    cols = lax.axis_size("across")
    pairs = []
    for i in range(rows):
        for j in range(cols):
            to = i - (step if j % 2 == 0 else -step)
            if 0 <= to < rows:
                pairs.append((i * cols + j, to * cols + j))
    return lax.ppermute(value, ("along", "across"), pairs)


def swap(value, first):
    count = lax.axis_size("across")
    pairs = []
    for i in range(first, count - 1, 2):
        pairs += [(i, i + 1), (i + 1, i)]
    return lax.ppermute(value, "across", pairs)


def vmem_out(*shapes):
    return [pltpu.VMEM(shape, dtype) for shape, dtype in shapes]


def pack_kernel(
    toa_in, seed_in, valid_in, cloud_in, land_in, row_in, col_in, tau_in, adjacency_in,
    early, late, outer, inner, cells, toa, row_taps, col_taps, scales,
    seed, valid, cloud, land, tau, adjacency, spot, sems,
):
    moves = [
        (seed_in, seed),
        (valid_in, valid),
        (cloud_in, cloud),
        (land_in, land),
        (toa_in, toa),
        (row_in, row_taps),
        (col_in, col_taps),
        (tau_in, tau),
        (adjacency_in, adjacency),
    ]
    copies = [pltpu.make_async_copy(x, y, sems.at[i]) for i, (x, y) in enumerate(moves)]
    for copy in copies:
        copy.start()
    for copy in copies[:4]:
        copy.wait()
    core = lax.rem(lax.axis_index("across"), 2)
    sub = iota((8, 128), 0)
    lane = iota((8, 128), 1)
    lane_at = iota((16, 128), 1)
    row_at = iota((16, 128), 0)
    whole = seed[...]
    high = whole.astype(BF16).astype(F32)
    rest = whole - high
    middle = rest.astype(BF16).astype(F32)
    conf = (valid[...] * (1 - cloud[...])).astype(F32)
    values = [high, middle, rest - middle, conf, land[...].astype(F32)]
    blank = jnp.zeros((8, 128), F32)
    spot[...] = jnp.zeros_like(spot)
    tiles = []
    for v in range(5):
        spot[0:CELL_ROWS, 4 : 4 + CELL_COLS] = values[v]
        base = spot[...]
        wide = jnp.where(
            lane < 4,
            pltpu.roll(base, 120, 1),
            jnp.where(lane < 12, base, jnp.where(lane < 16, pltpu.roll(base, 8, 1), 0.0)),
        )
        turned = pltpu.roll(wide, 6, 0)
        head = jnp.where(sub < 4, turned, 0.0)
        tile = jnp.concatenate([jnp.where(sub >= 6, turned, 0.0), head], axis=0)
        cells[v] = tile
        tiles.append(
            (
                jnp.concatenate([head, blank], axis=0).astype(BF16),
                jnp.concatenate([blank, pltpu.roll(wide, 4, 0)], axis=0).astype(BF16),
                tile.astype(BF16),
                pltpu.roll(tile, 112, 1).astype(BF16),
            )
        )
    copies[4].wait()

    def fill(go_down, go_up, to_left, to_right):
        go_down[...] = toa[:, ROWS - HALO :, :]
        go_up[...] = toa[:, :HALO, :]
        to_left[...] = toa[:, :, :SIDE]
        to_right[...] = toa[:, :, SIDE:]
        for v in range(5):
            first, last, left_cells, right_cells = tiles[v]
            for at in (0, 128):
                go_down[v, 0:16, at : at + 128] = jnp.where(
                    row_at < HALO - KR,
                    first,
                    toa[v, ROWS - HALO : ROWS - HALO + 16, at : at + 128],
                )
                go_up[v, HALO - 16 : HALO, at : at + 128] = jnp.where(
                    row_at >= 16 - (HALO - KR), last, toa[v, HALO - 16 : HALO, at : at + 128]
                )
            to_right[v, 0:16, :] = jnp.where(
                lane_at < SIDE - KR, left_cells, toa[v, 0:16, SIDE:]
            )
            to_left[v, 0:16, :] = jnp.where(lane_at < KR, toa[v, 0:16, 0:SIDE], right_cells)

    @pl.when(core == 0)
    def _():
        fill(late, early, outer, inner)

    @pl.when(core == 1)
    def _():
        fill(early, late, inner, outer)

    for copy in copies[5:]:
        copy.wait()
    for band in range(BANDS):
        scales[band : band + 1, :] = jnp.full((1, COLS), tau[band], F32)
        scales[8 + band : 9 + band, :] = jnp.full((1, COLS), adjacency[band], F32)


def pack(toa, seed, valid, cloud, land, row_taps, col_taps, tau, adjacency):
    cell = (CELL_ROWS, CELL_COLS)
    return pl.pallas_call(
        pack_kernel,
        in_specs=[pl.BlockSpec(memory_space=pltpu.HBM)] * 9,
        out_specs=[VMEM] * 9,
        out_shape=vmem_out(
            ((BANDS, HALO, COLS), BF16),
            ((BANDS, HALO, COLS), BF16),
            ((BANDS, ROWS, SIDE), BF16),
            ((BANDS, ROWS, SIDE), BF16),
            ((5, 16, 128), F32),
            ((BANDS, ROWS, COLS), BF16),
            ((BANDS, 3, TAPS), F32),
            ((BANDS, 3, TAPS), F32),
            ((16, COLS), F32),
        ),
        scratch_shapes=[
            pltpu.VMEM(cell, F32),
            pltpu.VMEM(cell, jnp.int32),
            pltpu.VMEM(cell, jnp.int32),
            pltpu.VMEM(cell, jnp.int32),
            pltpu.SMEM((BANDS,), F32),
            pltpu.SMEM((BANDS,), F32),
            pltpu.VMEM((8, 128), F32),
            pltpu.SemaphoreType.DMA((9,)),
        ],
        compiler_params=pltpu.CompilerParams(vmem_limit_bytes=58 << 20),
        name="pack",
    )(toa, seed, valid, cloud, land, row_taps, col_taps, tau, adjacency)


def toeplitz_kernel(row_ref, col_ref, near_out, far_out, col_out, pad_ref):
    pad_ref[...] = jnp.zeros_like(pad_ref)
    for band in range(BANDS):
        pad_ref[8 * band : 8 * band + 3, 4 : 4 + TAPS] = row_ref[band]
        pad_ref[8 * band + 4 : 8 * band + 7, 4 : 4 + TAPS] = col_ref[band]
    raw = pad_ref[...]
    total = jnp.sum(raw, axis=-1, keepdims=True)
    all_taps = (raw / jnp.where(total > 0.0, total, 1.0)).astype(BF16)
    flip = (iota((256, 256), 0) + iota((256, 256), 1) == TAPS + 7).astype(F32).astype(BF16)
    all_flipped = jnp.dot(all_taps, flip, preferred_element_type=F32)
    all_taps = all_taps.astype(F32)
    col_index = iota((384, 128), 1) - iota((384, 128), 0) + (SIDE + KR)
    col_good = (col_index >= 0) & (col_index < TAPS)
    row_at = iota((ROWS, 256), 1)
    row_base = row_at - iota((ROWS, 256), 0)
    near = row_base + KR
    near_good = (near >= 0) & (near < TAPS) & (row_at < ROWS)
    down_good = row_base + (ROWS + KR) < TAPS
    above = row_base - (2 * HALO - KR)
    above_good = (above >= 0) & (above < TAPS) & (row_at < 2 * HALO)

    def spread(vector, first):
        wide = jnp.broadcast_to(vector, (128, 256))
        return pltpu.roll(wide, first, 1, stride=1, stride_axis=0)

    def tall(value):
        swapped = jnp.concatenate([value[0:64, 128:256], value[0:64, 0:128]], axis=1)
        return jnp.concatenate([value, swapped], axis=0)

    for band in range(BANDS):
        for kern in range(3):
            at = 8 * band + 4 + kern
            rolled = spread(all_flipped[at : at + 1], 24)
            rolled = jnp.concatenate(
                [rolled[:, 0:128], rolled[:, 128:256], rolled[:, 0:128]], axis=0
            )
            tile = jnp.where(col_good, rolled, 0.0).astype(BF16)
            col_out[band, :, kern * 128 : (kern + 1) * 128] = tile
            vector = all_taps[8 * band + kern : 8 * band + kern + 1]
            part = slice(kern * ROWS, (kern + 1) * ROWS)
            near_out[band, part, :] = jnp.where(
                near_good, tall(spread(vector, 152)), 0.0
            ).astype(BF16)
            far_out[band, part, :] = jnp.where(
                down_good,
                tall(spread(vector, 216)),
                jnp.where(above_good, tall(spread(vector, HALO)), 0.0),
            ).astype(BF16)


def toeplitz(row_taps, col_taps):
    return pl.pallas_call(
        toeplitz_kernel,
        in_specs=[VMEM] * 2,
        out_specs=[VMEM] * 3,
        out_shape=vmem_out(
            ((BANDS, 3 * ROWS, 256), BF16),
            ((BANDS, 3 * ROWS, 256), BF16),
            ((BANDS, 384, 384), BF16),
        ),
        scratch_shapes=[pltpu.VMEM((8 * BANDS, 256), F32)],
        cost_estimate=pl.CostEstimate(flops=0, bytes_accessed=8_000_000, transcendentals=0),
        compiler_params=pltpu.CompilerParams(vmem_limit_bytes=8 << 20),
        name="toeplitz",
    )(row_taps, col_taps)


def split_kernel(toa, early, late, pace, outer, inner, field):
    del pace
    core = lax.rem(lax.axis_index("across"), 2)

    def fill(up, down, left, right):
        left[:, 0:HALO] = down[:, :, 0:SIDE]
        left[:, HALO:] = up[:, :, 0:SIDE]
        right[:, 0:HALO] = down[:, :, SIDE:]
        right[:, HALO:] = up[:, :, SIDE:]
        field[:, ROWS : ROWS + HALO] = down[...]
        field[:, ROWS + HALO :] = up[...]

    @pl.when(core == 0)
    def _():
        fill(late, early, outer, inner)

    @pl.when(core == 1)
    def _():
        fill(early, late, inner, outer)

    field[:, 0:ROWS] = toa[...]


def split(toa, early, late, pace):
    shape = ((BANDS, 2 * HALO, SIDE), BF16)
    return pl.pallas_call(
        split_kernel,
        in_specs=[VMEM] * 4,
        out_specs=[VMEM] * 3,
        out_shape=vmem_out(shape, shape, ((BANDS, ROWS + 2 * HALO, COLS), BF16)),
        compiler_params=pltpu.CompilerParams(vmem_limit_bytes=4 << 20),
        name="split",
    )(toa, early, late, pace)


def middle_matrix(col_mat, band, kern):
    at = slice(kern * 128, (kern + 1) * 128)
    return jnp.concatenate([col_mat[band, 128:384, at], col_mat[band, 0:256, at]], axis=1)


def side_matrix(col_mat, band, kern):
    at = slice(kern * 128, (kern + 1) * 128)
    blank = jnp.zeros((128, 128), BF16)
    return jnp.concatenate(
        [
            jnp.concatenate([col_mat[band, 0:128, at], blank], axis=1),
            jnp.concatenate([blank, col_mat[band, 256:384, at]], axis=1),
        ],
        axis=0,
    )


def own_kernel(field, outer, inner, near_mat, col_mat, env, halo, passed):
    core = lax.rem(lax.axis_index("across"), 2)
    for slot in range(2):
        passed[slot, ROWS:256, :] = jnp.zeros((256 - ROWS, 3 * COLS), BF16)

    def columns(band):
        first = outer[band]
        second = inner[band]
        sides = jnp.concatenate(
            [jnp.where(core == 0, first, second), jnp.where(core == 0, second, first)], axis=1
        )
        for kern in range(3):
            at = slice(kern * COLS, (kern + 1) * COLS)
            middle = middle_matrix(col_mat, band, kern)
            value = jnp.dot(field[band], middle, preferred_element_type=F32)
            halo[band, :, at] = value[ROWS:]
            value = value[0:ROWS] + jnp.dot(
                sides, side_matrix(col_mat, band, kern), preferred_element_type=F32
            )
            passed[band % 2, 0:ROWS, at] = value.astype(BF16)

    def rows(band):
        for kern in range(3):
            at = slice(kern * COLS, (kern + 1) * COLS)
            env[band, :, at] = jnp.dot(
                near_mat[band, kern * ROWS : (kern + 1) * ROWS, :],
                passed[band % 2, :, at],
                preferred_element_type=F32,
            )

    columns(0)
    for band in range(BANDS):
        if band + 1 < BANDS:
            columns(band + 1)
        rows(band)


def own_part(field, outer, inner, near_mat, col_mat):
    flops = BANDS * 2 * (192 * 512 * 768 + 208 * 256 * 768 + 192 * 256 * 768)
    return pl.pallas_call(
        own_kernel,
        in_specs=[VMEM] * 5,
        out_specs=[VMEM] * 2,
        out_shape=vmem_out(
            ((BANDS, ROWS, 3 * COLS), F32), ((BANDS, 2 * HALO, 3 * COLS), F32)
        ),
        scratch_shapes=[pltpu.VMEM((2, 256, 3 * COLS), BF16)],
        cost_estimate=pl.CostEstimate(
            flops=flops, bytes_accessed=10_000_000, transcendentals=0
        ),
        compiler_params=pltpu.CompilerParams(vmem_limit_bytes=8 << 20),
        name="own_part",
    )(field, outer, inner, near_mat, col_mat)


def cell_state(core, cells, field, outer, inner, far_outer, far_inner):
    low_at = ROWS + HALO
    sub = iota((8, 128), 0)
    lane = iota((8, 128), 1)
    both = iota((16, 128), 1)
    parts = []
    for v in range(5):
        out_up = far_outer[v, HALO : HALO + 8, :].astype(F32)
        in_up = far_inner[v, HALO : HALO + 8, :].astype(F32)
        out_down = far_outer[v, HALO - 8 : HALO, :].astype(F32)
        in_down = far_inner[v, HALO - 8 : HALO, :].astype(F32)
        out_side = outer[v, 0:16, :].astype(F32)
        in_side = inner[v, 0:16, :].astype(F32)
        top = jnp.where(
            lane < 4,
            jnp.where(core == 0, out_up, in_up),
            jnp.where(lane < 12, field[v, low_at : low_at + 8, 0:128].astype(F32), jnp.where(core == 0, in_up, out_up)),
        )
        low = jnp.where(
            lane < 4,
            jnp.where(core == 0, out_down, in_down),
            jnp.where(
                lane < 12,
                field[v, low_at - 8 : low_at, 0:128].astype(F32),
                jnp.where(core == 0, in_down, out_down),
            ),
        )
        west = jnp.where(core == 0, out_side, in_side)
        east = pltpu.roll(jnp.where(core == 0, in_side, out_side), 16, 1)
        middle = jnp.where(both < 4, west, jnp.where(both < 12, cells[v], east))
        first = jnp.where(sub < 6, pltpu.roll(top, 2, 0), middle[0:8])
        second = jnp.where(sub < 4, middle[8:16], low)
        parts.append(jnp.concatenate([first, second], axis=0))
    seed = parts[0] + parts[1] + parts[2]
    conf = parts[3]
    kind = parts[4]
    prior = jnp.where(kind < 0.5, 0.06, jnp.where(kind < 1.5, 0.2, 0.45))
    row = lax.axis_index("along") * CELL_ROWS + iota((16, 128), 0) - 6
    col = lax.axis_index("across") * CELL_COLS + iota((16, 128), 1) - 4
    last_row = lax.axis_size("along") * CELL_ROWS - 1
    last_col = lax.axis_size("across") * CELL_COLS - 1
    inside = (row >= 0) & (row <= last_row) & (col >= 0) & (col <= last_col)
    count = (
        (row > 0).astype(F32)
        + (row < last_row).astype(F32)
        + (col > 0).astype(F32)
        + (col < last_col).astype(F32)
    )
    count = jnp.maximum(count, 1.0)
    fix = conf * seed + (1.0 - conf) * (0.3 * prior)
    mult = 0.7 * (1.0 - conf)
    aot = jnp.where(inside, conf * seed + (1.0 - conf) * prior, 0.0)
    for _ in range(SWEEPS):
        near = (
            pltpu.roll(aot, 15, 0)
            + pltpu.roll(aot, 1, 0)
            + pltpu.roll(aot, 127, 1)
            + pltpu.roll(aot, 1, 1)
        )
        aot = jnp.where(inside, fix + mult * (near / count), 0.0)
    return pltpu.roll(aot, 10, 0)[0:8]


def last_kernel(
    scales, field, outer, inner, cells, far_outer, far_inner,
    far_mat, col_mat, env, halo, out, passed, result, sems,
):
    core = lax.rem(lax.axis_index("across"), 2)
    for slot in range(2):
        passed[slot, 2 * HALO : 256, :] = jnp.zeros((256 - 2 * HALO, 3 * COLS), BF16)

    def columns(band):
        first = far_outer[band]
        second = far_inner[band]
        sides = jnp.concatenate(
            [jnp.where(core == 0, first, second), jnp.where(core == 0, second, first)], axis=1
        )
        for kern in range(3):
            at = slice(kern * COLS, (kern + 1) * COLS)
            value = jnp.dot(
                sides, side_matrix(col_mat, band, kern), preferred_element_type=F32
            )
            passed[band % 2, 0 : 2 * HALO, at] = (value + halo[band, :, at]).astype(BF16)

    columns(0)
    small = cell_state(core, cells, field, outer, inner, far_outer, far_inner)
    block = iota((8, COLS), 1) // CB
    aot = jnp.zeros((8, COLS), F32)
    for j in range(CELL_COLS):
        aot = jnp.where(block == j, small[:, 4 + j : 5 + j], aot)
    gauss = []
    for center in (0.1, 0.35, 0.7):
        offset = aot - center
        gauss.append(jnp.exp(-(offset * offset) / 0.08))
    total = gauss[0] + gauss[1] + gauss[2]
    weights = [value / total for value in gauss]

    def copy(band):
        return pltpu.make_async_copy(result.at[band], out.at[band], sems.at[band])

    for band in range(BANDS):
        if band + 1 < BANDS:
            columns(band + 1)
        growth = jnp.exp(scales[band : band + 1, :] * aot)
        strength = scales[8 + band : 9 + band, :]
        own = (1.0 + strength) * growth
        scaled = strength * growth
        factors = [scaled * value for value in weights]
        sums = [
            env[band, :, kern * COLS : (kern + 1) * COLS]
            + jnp.dot(
                far_mat[band, kern * ROWS : (kern + 1) * ROWS, :],
                passed[band % 2, :, kern * COLS : (kern + 1) * COLS],
                preferred_element_type=F32,
            )
            for kern in range(3)
        ]
        for i in range(CELL_ROWS):
            part = slice(i * CB, (i + 1) * CB)
            value = own[i : i + 1, :] * field[band, part, :].astype(F32)
            for kern in range(3):
                value = value - factors[kern][i : i + 1, :] * sums[kern][part, :]
            result[band, part, :] = value
        copy(band).start()
    for band in range(BANDS):
        copy(band).wait()


def last_part(scales, field, outer, inner, cells, far_outer, far_inner, far_mat, col_mat, env, halo):
    flops = BANDS * 2 * (208 * 256 * 768 + 192 * 256 * 768)
    return pl.pallas_call(
        last_kernel,
        in_specs=[VMEM] * 11,
        out_specs=pl.BlockSpec(memory_space=pl.ANY),
        out_shape=jax.ShapeDtypeStruct((BANDS, ROWS, COLS), F32),
        scratch_shapes=[
            pltpu.VMEM((2, 256, 3 * COLS), BF16),
            pltpu.VMEM((BANDS, ROWS, COLS), F32),
            pltpu.SemaphoreType.DMA((BANDS,)),
        ],
        cost_estimate=pl.CostEstimate(
            flops=flops, bytes_accessed=12_000_000, transcendentals=0
        ),
        compiler_params=pltpu.CompilerParams(vmem_limit_bytes=8 << 20),
        name="last_part",
    )(
        scales, field, outer, inner, cells, far_outer, far_inner,
        far_mat, col_mat, env, halo,
    )


def body(toa, aot_seed, valid, cloud, land_class, row_taps, col_taps, tau, adjacency):
    to_early, to_late, to_outer, to_inner, cells, toa, row_taps, col_taps, scales = pack(
        toa, aot_seed, valid, cloud, land_class, row_taps, col_taps, tau, adjacency
    )
    early = exchange(to_early, 1)
    late = exchange(to_late, -1)
    outer = swap(to_outer, 1)
    inner = swap(to_inner, 0)
    near_mat, far_mat, col_mat = toeplitz(row_taps, col_taps)
    far_to_outer, far_to_inner, field = split(toa, early, late, near_mat)
    far_outer = swap(far_to_outer, 1)
    far_inner = swap(far_to_inner, 0)
    env, halo = own_part(field, outer, inner, near_mat, col_mat)
    return last_part(
        scales, field, outer, inner, cells, far_outer, far_inner,
        far_mat, col_mat, env, halo,
    )


def solution(mesh):
    cells = P("along", "across")
    in_specs = (P(None, "along", "across"), cells, cells, cells, cells, P(), P(), P(), P())
    out_specs = P(None, "along", "across")
    return jax.shard_map(body, mesh=mesh, in_specs=in_specs, out_specs=out_specs, check_vma=False)
```

```python
import jax
import jax.numpy as jnp
from jax import lax
from jax.experimental import pallas as pl
from jax.experimental.pallas import tpu as pltpu
from jax.sharding import PartitionSpec as P

BANDS = 6
KR = 100
TAPS = 201
CB = 32
SWEEPS = 4
ROWS = 192
COLS = 256
HALO = 104
SIDE = 128
CELL_ROWS = 6
CELL_COLS = 8
GROUP = KR // (BANDS - 1)
F32 = jnp.float32
BF16 = jnp.bfloat16
VMEM = pl.BlockSpec(memory_space=pltpu.VMEM)


def iota(shape, dim):
    return lax.broadcasted_iota(jnp.int32, shape, dim)


def exchange(value, step):
    rows = lax.axis_size("along")
    cols = lax.axis_size("across")
    pairs = []
    for i in range(rows):
        for j in range(cols):
            to = i - (step if j % 2 == 0 else -step)
            if 0 <= to < rows:
                pairs.append((i * cols + j, to * cols + j))
    return lax.ppermute(value, ("along", "across"), pairs)


def swap(value, first):
    count = lax.axis_size("across")
    pairs = []
    for i in range(first, count - 1, 2):
        pairs += [(i, i + 1), (i + 1, i)]
    return lax.ppermute(value, "across", pairs)


def vmem_out(*shapes):
    return [pltpu.VMEM(shape, dtype) for shape, dtype in shapes]


def pack_kernel(
    toa_in, seed_in, valid_in, cloud_in, land_in, row_in, col_in, tau_in, adjacency_in,
    early, late, outer, inner, cells, toa, row_taps, col_taps, scales,
    seed, valid, cloud, land, tau, adjacency, spot, sems,
):
    moves = [
        (seed_in, seed),
        (valid_in, valid),
        (cloud_in, cloud),
        (land_in, land),
        (toa_in, toa),
        (row_in, row_taps),
        (col_in, col_taps),
        (tau_in, tau),
        (adjacency_in, adjacency),
    ]
    copies = [pltpu.make_async_copy(x, y, sems.at[i]) for i, (x, y) in enumerate(moves)]
    for copy in copies:
        copy.start()
    for copy in copies[:4]:
        copy.wait()
    core = lax.rem(lax.axis_index("across"), 2)
    sub = iota((8, 128), 0)
    lane = iota((8, 128), 1)
    lane_at = iota((16, 128), 1)
    row_at = iota((16, 128), 0)
    whole = seed[...]
    high = whole.astype(BF16).astype(F32)
    rest = whole - high
    middle = rest.astype(BF16).astype(F32)
    conf = (valid[...] * (1 - cloud[...])).astype(F32)
    values = [high, middle, rest - middle, conf, land[...].astype(F32)]
    blank = jnp.zeros((8, 128), F32)
    spot[...] = jnp.zeros_like(spot)
    tiles = []
    for v in range(5):
        spot[0:CELL_ROWS, 4 : 4 + CELL_COLS] = values[v]
        base = spot[...]
        wide = jnp.where(
            lane < 4,
            pltpu.roll(base, 120, 1),
            jnp.where(lane < 12, base, jnp.where(lane < 16, pltpu.roll(base, 8, 1), 0.0)),
        )
        turned = pltpu.roll(wide, 6, 0)
        head = jnp.where(sub < 4, turned, 0.0)
        tile = jnp.concatenate([jnp.where(sub >= 6, turned, 0.0), head], axis=0)
        cells[v] = tile
        tiles.append(
            (
                jnp.concatenate([head, blank], axis=0).astype(BF16),
                jnp.concatenate([blank, pltpu.roll(wide, 4, 0)], axis=0).astype(BF16),
                tile.astype(BF16),
                pltpu.roll(tile, 112, 1).astype(BF16),
            )
        )
    copies[4].wait()

    def fill(go_down, go_up, to_left, to_right):
        go_down[...] = toa[:, ROWS - HALO :, :]
        go_up[...] = toa[:, :HALO, :]
        to_left[...] = toa[:, :, :SIDE]
        to_right[...] = toa[:, :, SIDE:]
        for v in range(5):
            first, last, left_cells, right_cells = tiles[v]
            for at in (0, 128):
                go_down[v, 0:16, at : at + 128] = jnp.where(
                    row_at < HALO - KR,
                    first,
                    toa[v, ROWS - HALO : ROWS - HALO + 16, at : at + 128],
                )
                go_up[v, HALO - 16 : HALO, at : at + 128] = jnp.where(
                    row_at >= 16 - (HALO - KR), last, toa[v, HALO - 16 : HALO, at : at + 128]
                )
            to_right[v, 0:16, :] = jnp.where(
                lane_at < SIDE - KR, left_cells, toa[v, 0:16, SIDE:]
            )
            to_left[v, 0:16, :] = jnp.where(lane_at < KR, toa[v, 0:16, 0:SIDE], right_cells)

    @pl.when(core == 0)
    def _():
        fill(late, early, outer, inner)

    @pl.when(core == 1)
    def _():
        fill(early, late, inner, outer)

    for copy in copies[5:]:
        copy.wait()
    for band in range(BANDS):
        scales[band : band + 1, :] = jnp.full((1, COLS), tau[band], F32)
        scales[8 + band : 9 + band, :] = jnp.full((1, COLS), adjacency[band], F32)


def pack(toa, seed, valid, cloud, land, row_taps, col_taps, tau, adjacency):
    cell = (CELL_ROWS, CELL_COLS)
    return pl.pallas_call(
        pack_kernel,
        in_specs=[pl.BlockSpec(memory_space=pltpu.HBM)] * 9,
        out_specs=[VMEM] * 9,
        out_shape=vmem_out(
            ((BANDS, HALO, COLS), BF16),
            ((BANDS, HALO, COLS), BF16),
            ((BANDS, ROWS, SIDE), BF16),
            ((BANDS, ROWS, SIDE), BF16),
            ((5, 16, 128), F32),
            ((BANDS, ROWS, COLS), BF16),
            ((BANDS, 3, TAPS), F32),
            ((BANDS, 3, TAPS), F32),
            ((16, COLS), F32),
        ),
        scratch_shapes=[
            pltpu.VMEM(cell, F32),
            pltpu.VMEM(cell, jnp.int32),
            pltpu.VMEM(cell, jnp.int32),
            pltpu.VMEM(cell, jnp.int32),
            pltpu.SMEM((BANDS,), F32),
            pltpu.SMEM((BANDS,), F32),
            pltpu.VMEM((8, 128), F32),
            pltpu.SemaphoreType.DMA((9,)),
        ],
        compiler_params=pltpu.CompilerParams(vmem_limit_bytes=58 << 20),
        name="pack",
    )(toa, seed, valid, cloud, land, row_taps, col_taps, tau, adjacency)


def spread(vector, first):
    wide = jnp.broadcast_to(vector, (128, 256))
    return pltpu.roll(wide, first, 1, stride=1, stride_axis=0)


def tall(value):
    swapped = jnp.concatenate([value[0:64, 128:256], value[0:64, 0:128]], axis=1)
    return jnp.concatenate([value, swapped], axis=0)


def toeplitz_kernel(row_ref, col_ref, near_out, taps_out, col_out, pad_ref):
    pad_ref[...] = jnp.zeros_like(pad_ref)
    for band in range(BANDS):
        pad_ref[8 * band : 8 * band + 3, 4 : 4 + TAPS] = row_ref[band]
        pad_ref[8 * band + 4 : 8 * band + 7, 4 : 4 + TAPS] = col_ref[band]
    raw = pad_ref[...]
    total = jnp.sum(raw, axis=-1, keepdims=True)
    all_taps = (raw / jnp.where(total > 0.0, total, 1.0)).astype(BF16)
    flip = (iota((256, 256), 0) + iota((256, 256), 1) == TAPS + 7).astype(F32).astype(BF16)
    all_flipped = jnp.dot(all_taps, flip, preferred_element_type=F32)
    all_taps = all_taps.astype(F32)
    taps_out[...] = all_taps
    col_index = iota((384, 128), 1) - iota((384, 128), 0) + (SIDE + KR)
    col_good = (col_index >= 0) & (col_index < TAPS)
    row_at = iota((ROWS, 256), 1)
    row_base = row_at - iota((ROWS, 256), 0)
    near = row_base + KR
    near_good = (near >= 0) & (near < TAPS) & (row_at < ROWS)

    for band in range(BANDS):
        for kern in range(3):
            at = 8 * band + 4 + kern
            rolled = spread(all_flipped[at : at + 1], 24)
            rolled = jnp.concatenate(
                [rolled[:, 0:128], rolled[:, 128:256], rolled[:, 0:128]], axis=0
            )
            tile = jnp.where(col_good, rolled, 0.0).astype(BF16)
            col_out[band, :, kern * 128 : (kern + 1) * 128] = tile
            vector = all_taps[8 * band + kern : 8 * band + kern + 1]
            part = slice(kern * ROWS, (kern + 1) * ROWS)
            near_out[band, part, :] = jnp.where(
                near_good, tall(spread(vector, 152)), 0.0
            ).astype(BF16)


def toeplitz(row_taps, col_taps):
    return pl.pallas_call(
        toeplitz_kernel,
        in_specs=[VMEM] * 2,
        out_specs=[VMEM] * 3,
        out_shape=vmem_out(
            ((BANDS, 3 * ROWS, 256), BF16),
            ((8 * BANDS, 256), F32),
            ((BANDS, 384, 384), BF16),
        ),
        scratch_shapes=[pltpu.VMEM((8 * BANDS, 256), F32)],
        cost_estimate=pl.CostEstimate(flops=0, bytes_accessed=8_000_000, transcendentals=0),
        compiler_params=pltpu.CompilerParams(vmem_limit_bytes=8 << 20),
        name="toeplitz",
    )(row_taps, col_taps)


def split_kernel(toa, early, late, pace, outer, inner, field):
    del pace
    core = lax.rem(lax.axis_index("across"), 2)

    lane = iota((2 * HALO, SIDE), 1)
    row = iota((2 * HALO, SIDE), 0)
    spare = (row >= KR) & (row < 2 * HALO - KR)

    def squeeze(strip, at, keep):
        part = slice(at, at + SIDE)
        last = field[BANDS - 1, ROWS:, part].astype(F32)
        for band in range(BANDS - 1):
            moved = pltpu.roll(last, KR - GROUP * band, 1)
            kept = field[band, ROWS:, part].astype(F32)
            strip[band] = jnp.where(keep, kept, moved).astype(BF16)

    def fill(up, down, to_left, to_right):
        field[:, ROWS : ROWS + HALO] = down[...]
        field[:, ROWS + HALO :] = up[...]
        squeeze(to_left, 0, (lane < KR) | spare)
        squeeze(to_right, SIDE, (lane >= SIDE - KR) | spare)

    @pl.when(core == 0)
    def _():
        fill(late, early, outer, inner)

    @pl.when(core == 1)
    def _():
        fill(early, late, inner, outer)

    field[:, 0:ROWS] = toa[...]


def split(toa, early, late, pace):
    return pl.pallas_call(
        split_kernel,
        in_specs=[VMEM] * 4,
        out_specs=[VMEM] * 3,
        out_shape=vmem_out(
            ((BANDS - 1, 2 * HALO, SIDE), BF16),
            ((BANDS - 1, 2 * HALO, SIDE), BF16),
            ((BANDS, ROWS + 2 * HALO, COLS), BF16),
        ),
        compiler_params=pltpu.CompilerParams(vmem_limit_bytes=4 << 20),
        name="split",
    )(toa, early, late, pace)


def middle_matrix(col_mat, band, kern):
    at = slice(kern * 128, (kern + 1) * 128)
    return jnp.concatenate([col_mat[band, 128:384, at], col_mat[band, 0:256, at]], axis=1)


def side_matrix(col_mat, band, kern):
    at = slice(kern * 128, (kern + 1) * 128)
    blank = jnp.zeros((128, 128), BF16)
    return jnp.concatenate(
        [
            jnp.concatenate([col_mat[band, 0:128, at], blank], axis=1),
            jnp.concatenate([blank, col_mat[band, 256:384, at]], axis=1),
        ],
        axis=0,
    )


def own_kernel(field, outer, inner, near_mat, col_mat, taps, env, halo, far_out, passed):
    core = lax.rem(lax.axis_index("across"), 2)
    for slot in range(2):
        passed[slot, ROWS:256, :] = jnp.zeros((256 - ROWS, 3 * COLS), BF16)

    def columns(band):
        first = outer[band]
        second = inner[band]
        sides = jnp.concatenate(
            [jnp.where(core == 0, first, second), jnp.where(core == 0, second, first)], axis=1
        )
        for kern in range(3):
            at = slice(kern * COLS, (kern + 1) * COLS)
            middle = middle_matrix(col_mat, band, kern)
            value = jnp.dot(field[band], middle, preferred_element_type=F32)
            halo[band, :, at] = value[ROWS:]
            value = value[0:ROWS] + jnp.dot(
                sides, side_matrix(col_mat, band, kern), preferred_element_type=F32
            )
            passed[band % 2, 0:ROWS, at] = value.astype(BF16)

    row_at = iota((ROWS, 256), 1)
    row_base = row_at - iota((ROWS, 256), 0)
    down_good = row_base + (ROWS + KR) < TAPS
    above = row_base - (2 * HALO - KR)
    above_good = (above >= 0) & (above < TAPS) & (row_at < 2 * HALO)

    def far(band):
        for kern in range(3):
            vector = taps[8 * band + kern : 8 * band + kern + 1, :]
            far_out[band, kern * ROWS : (kern + 1) * ROWS, :] = jnp.where(
                down_good,
                tall(spread(vector, 216)),
                jnp.where(above_good, tall(spread(vector, HALO)), 0.0),
            ).astype(BF16)

    def rows(band):
        for kern in range(3):
            at = slice(kern * COLS, (kern + 1) * COLS)
            env[band, :, at] = jnp.dot(
                near_mat[band, kern * ROWS : (kern + 1) * ROWS, :],
                passed[band % 2, :, at],
                preferred_element_type=F32,
            )

    columns(0)
    for band in range(BANDS):
        if band + 1 < BANDS:
            columns(band + 1)
        far(band)
        rows(band)


def own_part(field, outer, inner, near_mat, col_mat, taps):
    flops = BANDS * 2 * (192 * 512 * 768 + 208 * 256 * 768 + 192 * 256 * 768)
    return pl.pallas_call(
        own_kernel,
        in_specs=[VMEM] * 6,
        out_specs=[VMEM] * 3,
        out_shape=vmem_out(
            ((BANDS, ROWS, 3 * COLS), F32),
            ((BANDS, 2 * HALO, 3 * COLS), F32),
            ((BANDS, 3 * ROWS, 256), BF16),
        ),
        scratch_shapes=[pltpu.VMEM((2, 256, 3 * COLS), BF16)],
        cost_estimate=pl.CostEstimate(
            flops=flops, bytes_accessed=10_000_000, transcendentals=0
        ),
        compiler_params=pltpu.CompilerParams(vmem_limit_bytes=8 << 20),
        name="own_part",
    )(field, outer, inner, near_mat, col_mat, taps)


def cell_state(core, cells, field, outer, inner, far_outer, far_inner):
    low_at = ROWS + HALO
    sub = iota((8, 128), 0)
    lane = iota((8, 128), 1)
    both = iota((16, 128), 1)
    parts = []
    for v in range(5):
        out_up = far_outer[v, HALO : HALO + 8, :].astype(F32)
        in_up = far_inner[v, HALO : HALO + 8, :].astype(F32)
        out_down = far_outer[v, HALO - 8 : HALO, :].astype(F32)
        in_down = far_inner[v, HALO - 8 : HALO, :].astype(F32)
        out_side = outer[v, 0:16, :].astype(F32)
        in_side = inner[v, 0:16, :].astype(F32)
        top = jnp.where(
            lane < 4,
            jnp.where(core == 0, out_up, in_up),
            jnp.where(lane < 12, field[v, low_at : low_at + 8, 0:128].astype(F32), jnp.where(core == 0, in_up, out_up)),
        )
        low = jnp.where(
            lane < 4,
            jnp.where(core == 0, out_down, in_down),
            jnp.where(
                lane < 12,
                field[v, low_at - 8 : low_at, 0:128].astype(F32),
                jnp.where(core == 0, in_down, out_down),
            ),
        )
        west = jnp.where(core == 0, out_side, in_side)
        east = pltpu.roll(jnp.where(core == 0, in_side, out_side), 16, 1)
        middle = jnp.where(both < 4, west, jnp.where(both < 12, cells[v], east))
        first = jnp.where(sub < 6, pltpu.roll(top, 2, 0), middle[0:8])
        second = jnp.where(sub < 4, middle[8:16], low)
        parts.append(jnp.concatenate([first, second], axis=0))
    seed = parts[0] + parts[1] + parts[2]
    conf = parts[3]
    kind = parts[4]
    prior = jnp.where(kind < 0.5, 0.06, jnp.where(kind < 1.5, 0.2, 0.45))
    row = lax.axis_index("along") * CELL_ROWS + iota((16, 128), 0) - 6
    col = lax.axis_index("across") * CELL_COLS + iota((16, 128), 1) - 4
    last_row = lax.axis_size("along") * CELL_ROWS - 1
    last_col = lax.axis_size("across") * CELL_COLS - 1
    inside = (row >= 0) & (row <= last_row) & (col >= 0) & (col <= last_col)
    count = (
        (row > 0).astype(F32)
        + (row < last_row).astype(F32)
        + (col > 0).astype(F32)
        + (col < last_col).astype(F32)
    )
    count = jnp.maximum(count, 1.0)
    fix = conf * seed + (1.0 - conf) * (0.3 * prior)
    mult = 0.7 * (1.0 - conf)
    aot = jnp.where(inside, conf * seed + (1.0 - conf) * prior, 0.0)
    for _ in range(SWEEPS):
        near = (
            pltpu.roll(aot, 15, 0)
            + pltpu.roll(aot, 1, 0)
            + pltpu.roll(aot, 127, 1)
            + pltpu.roll(aot, 1, 1)
        )
        aot = jnp.where(inside, fix + mult * (near / count), 0.0)
    return pltpu.roll(aot, 10, 0)[0:8]


def last_kernel(
    scales, field, outer, inner, cells, far_outer, far_inner,
    far_mat, col_mat, env, halo, out, passed, result, sems,
):
    core = lax.rem(lax.axis_index("across"), 2)
    for slot in range(2):
        passed[slot, 2 * HALO : 256, :] = jnp.zeros((256 - 2 * HALO, 3 * COLS), BF16)

    lane = iota((2 * HALO, SIDE), 1)

    def last_band(strip, start):
        value = jnp.zeros((2 * HALO, SIDE), F32)
        for band in range(BANDS - 1):
            moved = pltpu.roll(strip[band].astype(F32), SIDE - KR + GROUP * band, 1)
            value = jnp.where(lane >= start + GROUP * band, moved, value)
        return value.astype(BF16)

    def columns(band):
        if band + 1 < BANDS:
            first = far_outer[band]
            second = far_inner[band]
        else:
            first = last_band(far_outer, jnp.where(core == 0, SIDE - KR, 0))
            second = last_band(far_inner, jnp.where(core == 0, 0, SIDE - KR))
        sides = jnp.concatenate(
            [jnp.where(core == 0, first, second), jnp.where(core == 0, second, first)], axis=1
        )
        for kern in range(3):
            at = slice(kern * COLS, (kern + 1) * COLS)
            value = jnp.dot(
                sides, side_matrix(col_mat, band, kern), preferred_element_type=F32
            )
            passed[band % 2, 0 : 2 * HALO, at] = (value + halo[band, :, at]).astype(BF16)

    columns(0)
    small = cell_state(core, cells, field, outer, inner, far_outer, far_inner)
    block = iota((8, COLS), 1) // CB
    aot = jnp.zeros((8, COLS), F32)
    for j in range(CELL_COLS):
        aot = jnp.where(block == j, small[:, 4 + j : 5 + j], aot)
    gauss = []
    for center in (0.1, 0.35, 0.7):
        offset = aot - center
        gauss.append(jnp.exp(-(offset * offset) / 0.08))
    total = gauss[0] + gauss[1] + gauss[2]
    weights = [value / total for value in gauss]

    def copy(band):
        return pltpu.make_async_copy(result.at[band], out.at[band], sems.at[band])

    for band in range(BANDS):
        if band + 1 < BANDS:
            columns(band + 1)
        growth = jnp.exp(scales[band : band + 1, :] * aot)
        strength = scales[8 + band : 9 + band, :]
        own = (1.0 + strength) * growth
        scaled = strength * growth
        factors = [scaled * value for value in weights]
        sums = [
            env[band, :, kern * COLS : (kern + 1) * COLS]
            + jnp.dot(
                far_mat[band, kern * ROWS : (kern + 1) * ROWS, :],
                passed[band % 2, :, kern * COLS : (kern + 1) * COLS],
                preferred_element_type=F32,
            )
            for kern in range(3)
        ]
        for i in range(CELL_ROWS):
            part = slice(i * CB, (i + 1) * CB)
            value = own[i : i + 1, :] * field[band, part, :].astype(F32)
            for kern in range(3):
                value = value - factors[kern][i : i + 1, :] * sums[kern][part, :]
            result[band, part, :] = value
        copy(band).start()
    for band in range(BANDS):
        copy(band).wait()


def last_part(scales, field, outer, inner, cells, far_outer, far_inner, far_mat, col_mat, env, halo):
    flops = BANDS * 2 * (208 * 256 * 768 + 192 * 256 * 768)
    return pl.pallas_call(
        last_kernel,
        in_specs=[VMEM] * 11,
        out_specs=pl.BlockSpec(memory_space=pl.ANY),
        out_shape=jax.ShapeDtypeStruct((BANDS, ROWS, COLS), F32),
        scratch_shapes=[
            pltpu.VMEM((2, 256, 3 * COLS), BF16),
            pltpu.VMEM((BANDS, ROWS, COLS), F32),
            pltpu.SemaphoreType.DMA((BANDS,)),
        ],
        cost_estimate=pl.CostEstimate(
            flops=flops, bytes_accessed=12_000_000, transcendentals=0
        ),
        compiler_params=pltpu.CompilerParams(vmem_limit_bytes=8 << 20),
        name="last_part",
    )(
        scales, field, outer, inner, cells, far_outer, far_inner,
        far_mat, col_mat, env, halo,
    )


def body(toa, aot_seed, valid, cloud, land_class, row_taps, col_taps, tau, adjacency):
    to_early, to_late, to_outer, to_inner, cells, toa, row_taps, col_taps, scales = pack(
        toa, aot_seed, valid, cloud, land_class, row_taps, col_taps, tau, adjacency
    )
    early = exchange(to_early, 1)
    late = exchange(to_late, -1)
    outer = swap(to_outer, 1)
    inner = swap(to_inner, 0)
    near_mat, taps, col_mat = toeplitz(row_taps, col_taps)
    far_to_outer, far_to_inner, field = split(toa, early, late, near_mat)
    far_outer = swap(far_to_outer, 1)
    far_inner = swap(far_to_inner, 0)
    env, halo, far_mat = own_part(field, outer, inner, near_mat, col_mat, taps)
    return last_part(
        scales, field, outer, inner, cells, far_outer, far_inner,
        far_mat, col_mat, env, halo,
    )


def solution(mesh):
    cells = P("along", "across")
    in_specs = (P(None, "along", "across"), cells, cells, cells, cells, P(), P(), P(), P())
    out_specs = P(None, "along", "across")
    return jax.shard_map(body, mesh=mesh, in_specs=in_specs, out_specs=out_specs, check_vma=False)
```

```python
import jax
import jax.numpy as jnp
from jax import lax
from jax.experimental import pallas as pl
from jax.experimental.pallas import tpu as pltpu
from jax.sharding import PartitionSpec as P

BANDS = 6
KR = 100
TAPS = 201
CB = 32
SWEEPS = 4
ROWS = 192
COLS = 256
HALO = 104
SIDE = 128
CELL_ROWS = 6
CELL_COLS = 8
GROUP = KR // (BANDS - 1)
F32 = jnp.float32
BF16 = jnp.bfloat16
VMEM = pl.BlockSpec(memory_space=pltpu.VMEM)


def iota(shape, dim):
    return lax.broadcasted_iota(jnp.int32, shape, dim)


def exchange(value, step):
    rows = lax.axis_size("along")
    cols = lax.axis_size("across")
    pairs = []
    for i in range(rows):
        for j in range(cols):
            to = i - (step if j % 2 == 0 else -step)
            if 0 <= to < rows:
                pairs.append((i * cols + j, to * cols + j))
    return lax.ppermute(value, ("along", "across"), pairs)


def swap(value, first):
    count = lax.axis_size("across")
    pairs = []
    for i in range(first, count - 1, 2):
        pairs += [(i, i + 1), (i + 1, i)]
    return lax.ppermute(value, "across", pairs)


def vmem_out(*shapes):
    return [pltpu.VMEM(shape, dtype) for shape, dtype in shapes]


def pack_kernel(
    toa_in, seed_in, valid_in, cloud_in, land_in, row_in, col_in, tau_in, adjacency_in,
    early, late, outer, inner, cells, toa, row_taps, col_taps, scales,
    seed, valid, cloud, land, tau, adjacency, spot, sems,
):
    moves = [
        (seed_in, seed),
        (valid_in, valid),
        (cloud_in, cloud),
        (land_in, land),
        (toa_in, toa),
        (row_in, row_taps),
        (col_in, col_taps),
        (tau_in, tau),
        (adjacency_in, adjacency),
    ]
    copies = [pltpu.make_async_copy(x, y, sems.at[i]) for i, (x, y) in enumerate(moves)]
    for copy in copies:
        copy.start()
    for copy in copies[:4]:
        copy.wait()
    core = lax.rem(lax.axis_index("across"), 2)
    sub = iota((8, 128), 0)
    lane = iota((8, 128), 1)
    lane_at = iota((16, 128), 1)
    row_at = iota((16, 128), 0)
    whole = seed[...]
    high = whole.astype(BF16).astype(F32)
    rest = whole - high
    middle = rest.astype(BF16).astype(F32)
    conf = (valid[...] * (1 - cloud[...])).astype(F32)
    values = [high, middle, rest - middle, conf, land[...].astype(F32)]
    blank = jnp.zeros((8, 128), F32)
    spot[...] = jnp.zeros_like(spot)
    tiles = []
    for v in range(5):
        spot[0:CELL_ROWS, 4 : 4 + CELL_COLS] = values[v]
        base = spot[...]
        wide = jnp.where(
            lane < 4,
            pltpu.roll(base, 120, 1),
            jnp.where(lane < 12, base, jnp.where(lane < 16, pltpu.roll(base, 8, 1), 0.0)),
        )
        turned = pltpu.roll(wide, 6, 0)
        head = jnp.where(sub < 4, turned, 0.0)
        tile = jnp.concatenate([jnp.where(sub >= 6, turned, 0.0), head], axis=0)
        cells[v] = tile
        tiles.append(
            (
                jnp.concatenate([head, blank], axis=0).astype(BF16),
                jnp.concatenate([blank, pltpu.roll(wide, 4, 0)], axis=0).astype(BF16),
                tile.astype(BF16),
                pltpu.roll(tile, 112, 1).astype(BF16),
            )
        )
    copies[4].wait()

    def fill(go_down, go_up, to_left, to_right):
        go_down[...] = toa[:, ROWS - HALO :, :]
        go_up[...] = toa[:, :HALO, :]
        to_left[...] = toa[:, :, :SIDE]
        to_right[...] = toa[:, :, SIDE:]
        for v in range(5):
            first, last, left_cells, right_cells = tiles[v]
            for at in (0, 128):
                go_down[v, 0:16, at : at + 128] = jnp.where(
                    row_at < HALO - KR,
                    first,
                    toa[v, ROWS - HALO : ROWS - HALO + 16, at : at + 128],
                )
                go_up[v, HALO - 16 : HALO, at : at + 128] = jnp.where(
                    row_at >= 16 - (HALO - KR), last, toa[v, HALO - 16 : HALO, at : at + 128]
                )
            to_right[v, 0:16, :] = jnp.where(
                lane_at < SIDE - KR, left_cells, toa[v, 0:16, SIDE:]
            )
            to_left[v, 0:16, :] = jnp.where(lane_at < KR, toa[v, 0:16, 0:SIDE], right_cells)

    @pl.when(core == 0)
    def _():
        fill(late, early, outer, inner)

    @pl.when(core == 1)
    def _():
        fill(early, late, inner, outer)

    for copy in copies[5:]:
        copy.wait()
    for band in range(BANDS):
        scales[band : band + 1, :] = jnp.full((1, COLS), tau[band], F32)
        scales[8 + band : 9 + band, :] = jnp.full((1, COLS), adjacency[band], F32)


def pack(toa, seed, valid, cloud, land, row_taps, col_taps, tau, adjacency):
    cell = (CELL_ROWS, CELL_COLS)
    return pl.pallas_call(
        pack_kernel,
        in_specs=[pl.BlockSpec(memory_space=pltpu.HBM)] * 9,
        out_specs=[VMEM] * 9,
        out_shape=vmem_out(
            ((BANDS, HALO, COLS), BF16),
            ((BANDS, HALO, COLS), BF16),
            ((BANDS, ROWS, SIDE), BF16),
            ((BANDS, ROWS, SIDE), BF16),
            ((5, 16, 128), F32),
            ((BANDS, ROWS, COLS), BF16),
            ((BANDS, 3, TAPS), F32),
            ((BANDS, 3, TAPS), F32),
            ((16, COLS), F32),
        ),
        scratch_shapes=[
            pltpu.VMEM(cell, F32),
            pltpu.VMEM(cell, jnp.int32),
            pltpu.VMEM(cell, jnp.int32),
            pltpu.VMEM(cell, jnp.int32),
            pltpu.SMEM((BANDS,), F32),
            pltpu.SMEM((BANDS,), F32),
            pltpu.VMEM((8, 128), F32),
            pltpu.SemaphoreType.DMA((9,)),
        ],
        compiler_params=pltpu.CompilerParams(vmem_limit_bytes=58 << 20),
        name="pack",
    )(toa, seed, valid, cloud, land, row_taps, col_taps, tau, adjacency)


def spread(vector, first):
    wide = jnp.broadcast_to(vector, (128, 256))
    return pltpu.roll(wide, first, 1, stride=1, stride_axis=0)


def tall(value):
    swapped = jnp.concatenate([value[0:64, 128:256], value[0:64, 0:128]], axis=1)
    return jnp.concatenate([value, swapped], axis=0)


def toeplitz_kernel(row_ref, col_ref, near_out, taps_out, col_out, pad_ref):
    pad_ref[...] = jnp.zeros_like(pad_ref)
    for band in range(BANDS):
        pad_ref[8 * band : 8 * band + 3, 4 : 4 + TAPS] = row_ref[band]
        pad_ref[8 * band + 4 : 8 * band + 7, 4 : 4 + TAPS] = col_ref[band]
    raw = pad_ref[...]
    total = jnp.sum(raw, axis=-1, keepdims=True)
    all_taps = (raw / jnp.where(total > 0.0, total, 1.0)).astype(BF16)
    flip = (iota((256, 256), 0) + iota((256, 256), 1) == TAPS + 7).astype(F32).astype(BF16)
    all_flipped = jnp.dot(all_taps, flip, preferred_element_type=F32)
    all_taps = all_taps.astype(F32)
    taps_out[...] = all_taps
    col_index = iota((384, 128), 1) - iota((384, 128), 0) + (SIDE + KR)
    col_good = (col_index >= 0) & (col_index < TAPS)
    row_at = iota((ROWS, 256), 1)
    row_base = row_at - iota((ROWS, 256), 0)
    near = row_base + KR
    near_good = (near >= 0) & (near < TAPS) & (row_at < ROWS)

    for band in range(BANDS):
        for kern in range(3):
            at = 8 * band + 4 + kern
            rolled = spread(all_flipped[at : at + 1], 24)
            rolled = jnp.concatenate(
                [rolled[:, 0:128], rolled[:, 128:256], rolled[:, 0:128]], axis=0
            )
            tile = jnp.where(col_good, rolled, 0.0).astype(BF16)
            col_out[band, :, kern * 128 : (kern + 1) * 128] = tile
            vector = all_taps[8 * band + kern : 8 * band + kern + 1]
            part = slice(kern * ROWS, (kern + 1) * ROWS)
            near_out[band, part, :] = jnp.where(
                near_good, tall(spread(vector, 152)), 0.0
            ).astype(BF16)


def toeplitz(row_taps, col_taps):
    return pl.pallas_call(
        toeplitz_kernel,
        in_specs=[VMEM] * 2,
        out_specs=[VMEM] * 3,
        out_shape=vmem_out(
            ((BANDS, 3 * ROWS, 256), BF16),
            ((8 * BANDS, 256), F32),
            ((BANDS, 384, 384), BF16),
        ),
        scratch_shapes=[pltpu.VMEM((8 * BANDS, 256), F32)],
        cost_estimate=pl.CostEstimate(flops=0, bytes_accessed=8_000_000, transcendentals=0),
        compiler_params=pltpu.CompilerParams(vmem_limit_bytes=8 << 20),
        name="toeplitz",
    )(row_taps, col_taps)


def split_kernel(toa, early, late, outer, inner, field):
    core = lax.rem(lax.axis_index("across"), 2)

    lane = iota((2 * HALO, SIDE), 1)
    row = iota((2 * HALO, SIDE), 0)
    spare = (row >= KR) & (row < 2 * HALO - KR)

    def squeeze(strip, at, keep):
        part = slice(at, at + SIDE)
        last = field[BANDS - 1, ROWS:, part].astype(F32)
        for band in range(BANDS - 1):
            moved = pltpu.roll(last, KR - GROUP * band, 1)
            kept = field[band, ROWS:, part].astype(F32)
            strip[band] = jnp.where(keep, kept, moved).astype(BF16)

    def fill(up, down, to_left, to_right):
        field[:, ROWS : ROWS + HALO] = down[...]
        field[:, ROWS + HALO :] = up[...]
        squeeze(to_left, 0, (lane < KR) | spare)
        squeeze(to_right, SIDE, (lane >= SIDE - KR) | spare)

    @pl.when(core == 0)
    def _():
        fill(late, early, outer, inner)

    @pl.when(core == 1)
    def _():
        fill(early, late, inner, outer)

    field[:, 0:ROWS] = toa[...]


def split(toa, early, late):
    return pl.pallas_call(
        split_kernel,
        in_specs=[VMEM] * 3,
        out_specs=[VMEM] * 3,
        out_shape=vmem_out(
            ((BANDS - 1, 2 * HALO, SIDE), BF16),
            ((BANDS - 1, 2 * HALO, SIDE), BF16),
            ((BANDS, ROWS + 2 * HALO, COLS), BF16),
        ),
        compiler_params=pltpu.CompilerParams(vmem_limit_bytes=4 << 20),
        name="split",
    )(toa, early, late)


def middle_matrix(col_mat, band, kern):
    at = slice(kern * 128, (kern + 1) * 128)
    return jnp.concatenate([col_mat[band, 128:384, at], col_mat[band, 0:256, at]], axis=1)


def side_matrix(col_mat, band, kern):
    at = slice(kern * 128, (kern + 1) * 128)
    blank = jnp.zeros((128, 128), BF16)
    return jnp.concatenate(
        [
            jnp.concatenate([col_mat[band, 0:128, at], blank], axis=1),
            jnp.concatenate([blank, col_mat[band, 256:384, at]], axis=1),
        ],
        axis=0,
    )


def own_kernel(field, outer, inner, near_mat, col_mat, taps, env, halo, far_out, passed):
    core = lax.rem(lax.axis_index("across"), 2)
    for slot in range(2):
        passed[slot, ROWS:256, :] = jnp.zeros((256 - ROWS, 3 * COLS), BF16)

    def columns(band):
        first = outer[band]
        second = inner[band]
        sides = jnp.concatenate(
            [jnp.where(core == 0, first, second), jnp.where(core == 0, second, first)], axis=1
        )
        for kern in range(3):
            at = slice(kern * COLS, (kern + 1) * COLS)
            middle = middle_matrix(col_mat, band, kern)
            value = jnp.dot(field[band], middle, preferred_element_type=F32)
            halo[band, :, at] = value[ROWS:]
            value = value[0:ROWS] + jnp.dot(
                sides, side_matrix(col_mat, band, kern), preferred_element_type=F32
            )
            passed[band % 2, 0:ROWS, at] = value.astype(BF16)

    row_at = iota((ROWS, 256), 1)
    row_base = row_at - iota((ROWS, 256), 0)
    down_good = row_base + (ROWS + KR) < TAPS
    above = row_base - (2 * HALO - KR)
    above_good = (above >= 0) & (above < TAPS) & (row_at < 2 * HALO)

    def far(band):
        for kern in range(3):
            vector = taps[8 * band + kern : 8 * band + kern + 1, :]
            far_out[band, kern * ROWS : (kern + 1) * ROWS, :] = jnp.where(
                down_good,
                tall(spread(vector, 216)),
                jnp.where(above_good, tall(spread(vector, HALO)), 0.0),
            ).astype(BF16)

    def rows(band):
        for kern in range(3):
            at = slice(kern * COLS, (kern + 1) * COLS)
            env[band, :, at] = jnp.dot(
                near_mat[band, kern * ROWS : (kern + 1) * ROWS, :],
                passed[band % 2, :, at],
                preferred_element_type=F32,
            )

    columns(0)
    for band in range(BANDS):
        if band + 1 < BANDS:
            columns(band + 1)
        far(band)
        rows(band)


def own_part(field, outer, inner, near_mat, col_mat, taps):
    flops = BANDS * 2 * (192 * 512 * 768 + 208 * 256 * 768 + 192 * 256 * 768)
    return pl.pallas_call(
        own_kernel,
        in_specs=[VMEM] * 6,
        out_specs=[VMEM] * 3,
        out_shape=vmem_out(
            ((BANDS, ROWS, 3 * COLS), F32),
            ((BANDS, 2 * HALO, 3 * COLS), F32),
            ((BANDS, 3 * ROWS, 256), BF16),
        ),
        scratch_shapes=[pltpu.VMEM((2, 256, 3 * COLS), BF16)],
        cost_estimate=pl.CostEstimate(
            flops=flops, bytes_accessed=10_000_000, transcendentals=0
        ),
        compiler_params=pltpu.CompilerParams(vmem_limit_bytes=8 << 20),
        name="own_part",
    )(field, outer, inner, near_mat, col_mat, taps)


def cell_state(core, cells, field, outer, inner, far_outer, far_inner):
    low_at = ROWS + HALO
    sub = iota((8, 128), 0)
    lane = iota((8, 128), 1)
    both = iota((16, 128), 1)
    parts = []
    for v in range(5):
        out_up = far_outer[v, HALO : HALO + 8, :].astype(F32)
        in_up = far_inner[v, HALO : HALO + 8, :].astype(F32)
        out_down = far_outer[v, HALO - 8 : HALO, :].astype(F32)
        in_down = far_inner[v, HALO - 8 : HALO, :].astype(F32)
        out_side = outer[v, 0:16, :].astype(F32)
        in_side = inner[v, 0:16, :].astype(F32)
        top = jnp.where(
            lane < 4,
            jnp.where(core == 0, out_up, in_up),
            jnp.where(lane < 12, field[v, low_at : low_at + 8, 0:128].astype(F32), jnp.where(core == 0, in_up, out_up)),
        )
        low = jnp.where(
            lane < 4,
            jnp.where(core == 0, out_down, in_down),
            jnp.where(
                lane < 12,
                field[v, low_at - 8 : low_at, 0:128].astype(F32),
                jnp.where(core == 0, in_down, out_down),
            ),
        )
        west = jnp.where(core == 0, out_side, in_side)
        east = pltpu.roll(jnp.where(core == 0, in_side, out_side), 16, 1)
        middle = jnp.where(both < 4, west, jnp.where(both < 12, cells[v], east))
        first = jnp.where(sub < 6, pltpu.roll(top, 2, 0), middle[0:8])
        second = jnp.where(sub < 4, middle[8:16], low)
        parts.append(jnp.concatenate([first, second], axis=0))
    seed = parts[0] + parts[1] + parts[2]
    conf = parts[3]
    kind = parts[4]
    prior = jnp.where(kind < 0.5, 0.06, jnp.where(kind < 1.5, 0.2, 0.45))
    row = lax.axis_index("along") * CELL_ROWS + iota((16, 128), 0) - 6
    col = lax.axis_index("across") * CELL_COLS + iota((16, 128), 1) - 4
    last_row = lax.axis_size("along") * CELL_ROWS - 1
    last_col = lax.axis_size("across") * CELL_COLS - 1
    inside = (row >= 0) & (row <= last_row) & (col >= 0) & (col <= last_col)
    count = (
        (row > 0).astype(F32)
        + (row < last_row).astype(F32)
        + (col > 0).astype(F32)
        + (col < last_col).astype(F32)
    )
    count = jnp.maximum(count, 1.0)
    fix = conf * seed + (1.0 - conf) * (0.3 * prior)
    mult = 0.7 * (1.0 - conf)
    aot = jnp.where(inside, conf * seed + (1.0 - conf) * prior, 0.0)
    for _ in range(SWEEPS):
        near = (
            pltpu.roll(aot, 15, 0)
            + pltpu.roll(aot, 1, 0)
            + pltpu.roll(aot, 127, 1)
            + pltpu.roll(aot, 1, 1)
        )
        aot = jnp.where(inside, fix + mult * (near / count), 0.0)
    return pltpu.roll(aot, 10, 0)[0:8]


def last_kernel(
    scales, field, outer, inner, cells, far_outer, far_inner,
    far_mat, col_mat, env, halo, out, passed, result, sems,
):
    core = lax.rem(lax.axis_index("across"), 2)
    for slot in range(2):
        passed[slot, 2 * HALO : 256, :] = jnp.zeros((256 - 2 * HALO, 3 * COLS), BF16)

    lane = iota((2 * HALO, SIDE), 1)

    def last_band(strip, start):
        value = jnp.zeros((2 * HALO, SIDE), F32)
        for band in range(BANDS - 1):
            moved = pltpu.roll(strip[band].astype(F32), SIDE - KR + GROUP * band, 1)
            value = jnp.where(lane >= start + GROUP * band, moved, value)
        return value.astype(BF16)

    def columns(band):
        if band + 1 < BANDS:
            first = far_outer[band]
            second = far_inner[band]
        else:
            first = last_band(far_outer, jnp.where(core == 0, SIDE - KR, 0))
            second = last_band(far_inner, jnp.where(core == 0, 0, SIDE - KR))
        sides = jnp.concatenate(
            [jnp.where(core == 0, first, second), jnp.where(core == 0, second, first)], axis=1
        )
        for kern in range(3):
            at = slice(kern * COLS, (kern + 1) * COLS)
            value = jnp.dot(
                sides, side_matrix(col_mat, band, kern), preferred_element_type=F32
            )
            passed[band % 2, 0 : 2 * HALO, at] = (value + halo[band, :, at]).astype(BF16)

    columns(0)
    small = cell_state(core, cells, field, outer, inner, far_outer, far_inner)
    block = iota((8, COLS), 1) // CB
    aot = jnp.zeros((8, COLS), F32)
    for j in range(CELL_COLS):
        aot = jnp.where(block == j, small[:, 4 + j : 5 + j], aot)
    gauss = []
    for center in (0.1, 0.35, 0.7):
        offset = aot - center
        gauss.append(jnp.exp(-(offset * offset) / 0.08))
    total = gauss[0] + gauss[1] + gauss[2]
    weights = [value / total for value in gauss]

    def copy(band):
        return pltpu.make_async_copy(result.at[band], out.at[band], sems.at[band])

    for band in range(BANDS):
        if band + 1 < BANDS:
            columns(band + 1)
        growth = jnp.exp(scales[band : band + 1, :] * aot)
        strength = scales[8 + band : 9 + band, :]
        own = (1.0 + strength) * growth
        scaled = strength * growth
        factors = [scaled * value for value in weights]
        sums = [
            env[band, :, kern * COLS : (kern + 1) * COLS]
            + jnp.dot(
                far_mat[band, kern * ROWS : (kern + 1) * ROWS, :],
                passed[band % 2, :, kern * COLS : (kern + 1) * COLS],
                preferred_element_type=F32,
            )
            for kern in range(3)
        ]
        for i in range(CELL_ROWS):
            part = slice(i * CB, (i + 1) * CB)
            value = own[i : i + 1, :] * field[band, part, :].astype(F32)
            for kern in range(3):
                value = value - factors[kern][i : i + 1, :] * sums[kern][part, :]
            result[band, part, :] = value
        copy(band).start()
    for band in range(BANDS):
        copy(band).wait()


def last_part(scales, field, outer, inner, cells, far_outer, far_inner, far_mat, col_mat, env, halo):
    flops = BANDS * 2 * (208 * 256 * 768 + 192 * 256 * 768)
    return pl.pallas_call(
        last_kernel,
        in_specs=[VMEM] * 11,
        out_specs=pl.BlockSpec(memory_space=pl.ANY),
        out_shape=jax.ShapeDtypeStruct((BANDS, ROWS, COLS), F32),
        scratch_shapes=[
            pltpu.VMEM((2, 256, 3 * COLS), BF16),
            pltpu.VMEM((BANDS, ROWS, COLS), F32),
            pltpu.SemaphoreType.DMA((BANDS,)),
        ],
        cost_estimate=pl.CostEstimate(
            flops=flops, bytes_accessed=12_000_000, transcendentals=0
        ),
        compiler_params=pltpu.CompilerParams(vmem_limit_bytes=8 << 20),
        name="last_part",
    )(
        scales, field, outer, inner, cells, far_outer, far_inner,
        far_mat, col_mat, env, halo,
    )


def body(toa, aot_seed, valid, cloud, land_class, row_taps, col_taps, tau, adjacency):
    to_early, to_late, to_outer, to_inner, cells, toa, row_taps, col_taps, scales = pack(
        toa, aot_seed, valid, cloud, land_class, row_taps, col_taps, tau, adjacency
    )
    early = exchange(to_early, 1)
    late = exchange(to_late, -1)
    outer = swap(to_outer, 1)
    inner = swap(to_inner, 0)
    near_mat, taps, col_mat = toeplitz(row_taps, col_taps)
    far_to_outer, far_to_inner, field = split(toa, early, late)
    far_outer = swap(far_to_outer, 1)
    far_inner = swap(far_to_inner, 0)
    env, halo, far_mat = own_part(field, outer, inner, near_mat, col_mat, taps)
    return last_part(
        scales, field, outer, inner, cells, far_outer, far_inner,
        far_mat, col_mat, env, halo,
    )


def solution(mesh):
    cells = P("along", "across")
    in_specs = (P(None, "along", "across"), cells, cells, cells, cells, P(), P(), P(), P())
    out_specs = P(None, "along", "across")
    return jax.shard_map(body, mesh=mesh, in_specs=in_specs, out_specs=out_specs, check_vma=False)
```

```python
import jax
import jax.numpy as jnp
from jax import lax
from jax.experimental import pallas as pl
from jax.experimental.pallas import tpu as pltpu
from jax.sharding import PartitionSpec as P

BANDS = 6
KR = 100
TAPS = 201
CB = 32
SWEEPS = 4
ROWS = 192
COLS = 256
HALO = 104
SIDE = 128
CELL_ROWS = 6
CELL_COLS = 8
GROUP = KR // (BANDS - 1)
F32 = jnp.float32
BF16 = jnp.bfloat16
VMEM = pl.BlockSpec(memory_space=pltpu.VMEM)


def iota(shape, dim):
    return lax.broadcasted_iota(jnp.int32, shape, dim)


def exchange(value, step):
    rows = lax.axis_size("along")
    cols = lax.axis_size("across")
    pairs = []
    for i in range(rows):
        for j in range(cols):
            to = i - (step if j % 2 == 0 else -step)
            if 0 <= to < rows:
                pairs.append((i * cols + j, to * cols + j))
    return lax.ppermute(value, ("along", "across"), pairs)


def swap(value, first):
    count = lax.axis_size("across")
    pairs = []
    for i in range(first, count - 1, 2):
        pairs += [(i, i + 1), (i + 1, i)]
    return lax.ppermute(value, "across", pairs)


def vmem_out(*shapes):
    return [pltpu.VMEM(shape, dtype) for shape, dtype in shapes]


def pack_kernel(
    toa_in, seed_in, valid_in, cloud_in, land_in, row_in, col_in, tau_in, adjacency_in,
    early, late, outer, inner, cells, toa, row_taps, col_taps, scales,
    seed, valid, cloud, land, tau, adjacency, spot, sems,
):
    moves = [
        (seed_in, seed),
        (valid_in, valid),
        (cloud_in, cloud),
        (land_in, land),
        (toa_in, toa),
        (row_in, row_taps),
        (col_in, col_taps),
        (tau_in, tau),
        (adjacency_in, adjacency),
    ]
    copies = [pltpu.make_async_copy(x, y, sems.at[i]) for i, (x, y) in enumerate(moves)]
    for copy in copies:
        copy.start()
    for copy in copies[:4]:
        copy.wait()
    core = lax.rem(lax.axis_index("across"), 2)
    sub = iota((8, 128), 0)
    lane = iota((8, 128), 1)
    lane_at = iota((16, 128), 1)
    row_at = iota((16, 128), 0)
    whole = seed[...]
    high = whole.astype(BF16).astype(F32)
    rest = whole - high
    middle = rest.astype(BF16).astype(F32)
    conf = (valid[...] * (1 - cloud[...])).astype(F32)
    values = [high, middle, rest - middle, conf, land[...].astype(F32)]
    blank = jnp.zeros((8, 128), F32)
    spot[...] = jnp.zeros_like(spot)
    tiles = []
    for v in range(5):
        spot[0:CELL_ROWS, 4 : 4 + CELL_COLS] = values[v]
        base = spot[...]
        wide = jnp.where(
            lane < 4,
            pltpu.roll(base, 120, 1),
            jnp.where(lane < 12, base, jnp.where(lane < 16, pltpu.roll(base, 8, 1), 0.0)),
        )
        turned = pltpu.roll(wide, 6, 0)
        head = jnp.where(sub < 4, turned, 0.0)
        tile = jnp.concatenate([jnp.where(sub >= 6, turned, 0.0), head], axis=0)
        cells[v] = tile
        tiles.append(
            (
                jnp.concatenate([head, blank], axis=0).astype(BF16),
                jnp.concatenate([blank, pltpu.roll(wide, 4, 0)], axis=0).astype(BF16),
                tile.astype(BF16),
                pltpu.roll(tile, 112, 1).astype(BF16),
            )
        )
    copies[4].wait()

    def fill(go_down, go_up, to_left, to_right):
        go_down[...] = toa[:, ROWS - HALO :, :]
        go_up[...] = toa[:, :HALO, :]
        to_left[...] = toa[:, :, :SIDE]
        to_right[...] = toa[:, :, SIDE:]
        for v in range(5):
            first, last, left_cells, right_cells = tiles[v]
            for at in (0, 128):
                go_down[v, 0:16, at : at + 128] = jnp.where(
                    row_at < HALO - KR,
                    first,
                    toa[v, ROWS - HALO : ROWS - HALO + 16, at : at + 128],
                )
                go_up[v, HALO - 16 : HALO, at : at + 128] = jnp.where(
                    row_at >= 16 - (HALO - KR), last, toa[v, HALO - 16 : HALO, at : at + 128]
                )
            to_right[v, 0:16, :] = jnp.where(
                lane_at < SIDE - KR, left_cells, toa[v, 0:16, SIDE:]
            )
            to_left[v, 0:16, :] = jnp.where(lane_at < KR, toa[v, 0:16, 0:SIDE], right_cells)

    @pl.when(core == 0)
    def _():
        fill(late, early, outer, inner)

    @pl.when(core == 1)
    def _():
        fill(early, late, inner, outer)

    for copy in copies[5:]:
        copy.wait()
    for band in range(BANDS):
        scales[band : band + 1, :] = jnp.full((1, COLS), tau[band], F32)
        scales[8 + band : 9 + band, :] = jnp.full((1, COLS), adjacency[band], F32)


def pack(toa, seed, valid, cloud, land, row_taps, col_taps, tau, adjacency):
    cell = (CELL_ROWS, CELL_COLS)
    return pl.pallas_call(
        pack_kernel,
        in_specs=[pl.BlockSpec(memory_space=pltpu.HBM)] * 9,
        out_specs=[VMEM] * 9,
        out_shape=vmem_out(
            ((BANDS, HALO, COLS), BF16),
            ((BANDS, HALO, COLS), BF16),
            ((BANDS, ROWS, SIDE), BF16),
            ((BANDS, ROWS, SIDE), BF16),
            ((5, 16, 128), F32),
            ((BANDS, ROWS, COLS), BF16),
            ((BANDS, 3, TAPS), F32),
            ((BANDS, 3, TAPS), F32),
            ((16, COLS), F32),
        ),
        scratch_shapes=[
            pltpu.VMEM(cell, F32),
            pltpu.VMEM(cell, jnp.int32),
            pltpu.VMEM(cell, jnp.int32),
            pltpu.VMEM(cell, jnp.int32),
            pltpu.SMEM((BANDS,), F32),
            pltpu.SMEM((BANDS,), F32),
            pltpu.VMEM((8, 128), F32),
            pltpu.SemaphoreType.DMA((9,)),
        ],
        compiler_params=pltpu.CompilerParams(vmem_limit_bytes=58 << 20),
        name="pack",
    )(toa, seed, valid, cloud, land, row_taps, col_taps, tau, adjacency)


def spread(vector, first):
    wide = jnp.broadcast_to(vector, (128, 256))
    return pltpu.roll(wide, first, 1, stride=1, stride_axis=0)


def tall(value):
    swapped = jnp.concatenate([value[0:64, 128:256], value[0:64, 0:128]], axis=1)
    return jnp.concatenate([value, swapped], axis=0)


def toeplitz_kernel(row_ref, col_ref, near_out, taps_out, col_out, pad_ref):
    pad_ref[...] = jnp.zeros_like(pad_ref)
    for band in range(BANDS):
        pad_ref[8 * band : 8 * band + 3, 4 : 4 + TAPS] = row_ref[band]
        pad_ref[8 * band + 4 : 8 * band + 7, 4 : 4 + TAPS] = col_ref[band]
    raw = pad_ref[...]
    total = jnp.sum(raw, axis=-1, keepdims=True)
    all_taps = (raw / jnp.where(total > 0.0, total, 1.0)).astype(BF16)
    flip = (iota((256, 256), 0) + iota((256, 256), 1) == TAPS + 7).astype(F32).astype(BF16)
    all_flipped = jnp.dot(all_taps, flip, preferred_element_type=F32)
    all_taps = all_taps.astype(F32)
    taps_out[...] = all_taps
    col_index = iota((384, 128), 1) - iota((384, 128), 0) + (SIDE + KR)
    col_good = (col_index >= 0) & (col_index < TAPS)
    row_at = iota((ROWS, 256), 1)
    row_base = row_at - iota((ROWS, 256), 0)
    near = row_base + KR
    near_good = (near >= 0) & (near < TAPS) & (row_at < ROWS)

    for band in range(BANDS):
        for kern in range(3):
            at = 8 * band + 4 + kern
            rolled = spread(all_flipped[at : at + 1], 24)
            rolled = jnp.concatenate(
                [rolled[:, 0:128], rolled[:, 128:256], rolled[:, 0:128]], axis=0
            )
            tile = jnp.where(col_good, rolled, 0.0).astype(BF16)
            col_out[band, :, kern * 128 : (kern + 1) * 128] = tile
            vector = all_taps[8 * band + kern : 8 * band + kern + 1]
            part = slice(kern * ROWS, (kern + 1) * ROWS)
            near_out[band, part, :] = jnp.where(
                near_good, tall(spread(vector, 152)), 0.0
            ).astype(BF16)


def toeplitz(row_taps, col_taps):
    return pl.pallas_call(
        toeplitz_kernel,
        in_specs=[VMEM] * 2,
        out_specs=[VMEM] * 3,
        out_shape=vmem_out(
            ((BANDS, 3 * ROWS, 256), BF16),
            ((8 * BANDS, 256), F32),
            ((BANDS, 384, 384), BF16),
        ),
        scratch_shapes=[pltpu.VMEM((8 * BANDS, 256), F32)],
        cost_estimate=pl.CostEstimate(flops=0, bytes_accessed=8_000_000, transcendentals=0),
        compiler_params=pltpu.CompilerParams(vmem_limit_bytes=8 << 20),
        name="toeplitz",
    )(row_taps, col_taps)


def split_kernel(toa, early, late, outer, inner, field):
    core = lax.rem(lax.axis_index("across"), 2)

    lane = iota((2 * HALO, SIDE), 1)
    row = iota((2 * HALO, SIDE), 0)
    spare = (row >= KR) & (row < 2 * HALO - KR)

    def squeeze(strip, at, keep):
        part = slice(at, at + SIDE)
        last = field[BANDS - 1, ROWS:, part].astype(F32)
        for band in range(BANDS - 1):
            moved = pltpu.roll(last, KR - GROUP * band, 1)
            kept = field[band, ROWS:, part].astype(F32)
            strip[band] = jnp.where(keep, kept, moved).astype(BF16)

    def fill(up, down, to_left, to_right):
        field[:, ROWS : ROWS + HALO] = down[...]
        field[:, ROWS + HALO :] = up[...]
        squeeze(to_left, 0, (lane < KR) | spare)
        squeeze(to_right, SIDE, (lane >= SIDE - KR) | spare)

    @pl.when(core == 0)
    def _():
        fill(late, early, outer, inner)

    @pl.when(core == 1)
    def _():
        fill(early, late, inner, outer)

    field[:, 0:ROWS] = toa[...]


def split(toa, early, late):
    return pl.pallas_call(
        split_kernel,
        in_specs=[VMEM] * 3,
        out_specs=[VMEM] * 3,
        out_shape=vmem_out(
            ((BANDS - 1, 2 * HALO, SIDE), BF16),
            ((BANDS - 1, 2 * HALO, SIDE), BF16),
            ((BANDS, ROWS + 2 * HALO, COLS), BF16),
        ),
        compiler_params=pltpu.CompilerParams(vmem_limit_bytes=4 << 20),
        name="split",
    )(toa, early, late)


def middle_matrix(col_mat, band, kern):
    at = slice(kern * 128, (kern + 1) * 128)
    return jnp.concatenate([col_mat[band, 128:384, at], col_mat[band, 0:256, at]], axis=1)


def side_matrix(col_mat, band, kern):
    at = slice(kern * 128, (kern + 1) * 128)
    blank = jnp.zeros((128, 128), BF16)
    return jnp.concatenate(
        [
            jnp.concatenate([col_mat[band, 0:128, at], blank], axis=1),
            jnp.concatenate([blank, col_mat[band, 256:384, at]], axis=1),
        ],
        axis=0,
    )


def own_kernel(field, outer, inner, near_mat, col_mat, taps, env, halo, far_out, passed):
    core = lax.rem(lax.axis_index("across"), 2)
    for slot in range(3):
        passed[slot, ROWS:256, :] = jnp.zeros((256 - ROWS, 3 * COLS), BF16)

    def columns(band):
        first = outer[band]
        second = inner[band]
        sides = jnp.concatenate(
            [jnp.where(core == 0, first, second), jnp.where(core == 0, second, first)], axis=1
        )
        for kern in range(3):
            at = slice(kern * COLS, (kern + 1) * COLS)
            middle = middle_matrix(col_mat, band, kern)
            value = jnp.dot(field[band], middle, preferred_element_type=F32)
            halo[band, :, at] = value[ROWS:]
            value = value[0:ROWS] + jnp.dot(
                sides, side_matrix(col_mat, band, kern), preferred_element_type=F32
            )
            passed[band % 3, 0:ROWS, at] = value.astype(BF16)

    row_at = iota((ROWS, 256), 1)
    row_base = row_at - iota((ROWS, 256), 0)
    down_good = row_base + (ROWS + KR) < TAPS
    above = row_base - (2 * HALO - KR)
    above_good = (above >= 0) & (above < TAPS) & (row_at < 2 * HALO)

    def far(band):
        for kern in range(3):
            vector = taps[8 * band + kern : 8 * band + kern + 1, :]
            far_out[band, kern * ROWS : (kern + 1) * ROWS, :] = jnp.where(
                down_good,
                tall(spread(vector, 216)),
                jnp.where(above_good, tall(spread(vector, HALO)), 0.0),
            ).astype(BF16)

    def rows(band):
        for kern in range(3):
            at = slice(kern * COLS, (kern + 1) * COLS)
            env[band, :, at] = jnp.dot(
                near_mat[band, kern * ROWS : (kern + 1) * ROWS, :],
                passed[band % 3, :, at],
                preferred_element_type=F32,
            )

    columns(0)
    columns(1)
    for band in range(BANDS):
        if band + 2 < BANDS:
            columns(band + 2)
        far(band)
        rows(band)


def own_part(field, outer, inner, near_mat, col_mat, taps):
    flops = BANDS * 2 * (192 * 512 * 768 + 208 * 256 * 768 + 192 * 256 * 768)
    return pl.pallas_call(
        own_kernel,
        in_specs=[VMEM] * 6,
        out_specs=[VMEM] * 3,
        out_shape=vmem_out(
            ((BANDS, ROWS, 3 * COLS), F32),
            ((BANDS, 2 * HALO, 3 * COLS), F32),
            ((BANDS, 3 * ROWS, 256), BF16),
        ),
        scratch_shapes=[pltpu.VMEM((3, 256, 3 * COLS), BF16)],
        cost_estimate=pl.CostEstimate(
            flops=flops, bytes_accessed=10_000_000, transcendentals=0
        ),
        compiler_params=pltpu.CompilerParams(vmem_limit_bytes=8 << 20),
        name="own_part",
    )(field, outer, inner, near_mat, col_mat, taps)


def cell_state(core, cells, field, outer, inner, far_outer, far_inner):
    low_at = ROWS + HALO
    sub = iota((8, 128), 0)
    lane = iota((8, 128), 1)
    both = iota((16, 128), 1)
    parts = []
    for v in range(5):
        out_up = far_outer[v, HALO : HALO + 8, :].astype(F32)
        in_up = far_inner[v, HALO : HALO + 8, :].astype(F32)
        out_down = far_outer[v, HALO - 8 : HALO, :].astype(F32)
        in_down = far_inner[v, HALO - 8 : HALO, :].astype(F32)
        out_side = outer[v, 0:16, :].astype(F32)
        in_side = inner[v, 0:16, :].astype(F32)
        top = jnp.where(
            lane < 4,
            jnp.where(core == 0, out_up, in_up),
            jnp.where(lane < 12, field[v, low_at : low_at + 8, 0:128].astype(F32), jnp.where(core == 0, in_up, out_up)),
        )
        low = jnp.where(
            lane < 4,
            jnp.where(core == 0, out_down, in_down),
            jnp.where(
                lane < 12,
                field[v, low_at - 8 : low_at, 0:128].astype(F32),
                jnp.where(core == 0, in_down, out_down),
            ),
        )
        west = jnp.where(core == 0, out_side, in_side)
        east = pltpu.roll(jnp.where(core == 0, in_side, out_side), 16, 1)
        middle = jnp.where(both < 4, west, jnp.where(both < 12, cells[v], east))
        first = jnp.where(sub < 6, pltpu.roll(top, 2, 0), middle[0:8])
        second = jnp.where(sub < 4, middle[8:16], low)
        parts.append(jnp.concatenate([first, second], axis=0))
    seed = parts[0] + parts[1] + parts[2]
    conf = parts[3]
    kind = parts[4]
    prior = jnp.where(kind < 0.5, 0.06, jnp.where(kind < 1.5, 0.2, 0.45))
    row = lax.axis_index("along") * CELL_ROWS + iota((16, 128), 0) - 6
    col = lax.axis_index("across") * CELL_COLS + iota((16, 128), 1) - 4
    last_row = lax.axis_size("along") * CELL_ROWS - 1
    last_col = lax.axis_size("across") * CELL_COLS - 1
    inside = (row >= 0) & (row <= last_row) & (col >= 0) & (col <= last_col)
    count = (
        (row > 0).astype(F32)
        + (row < last_row).astype(F32)
        + (col > 0).astype(F32)
        + (col < last_col).astype(F32)
    )
    count = jnp.maximum(count, 1.0)
    fix = conf * seed + (1.0 - conf) * (0.3 * prior)
    mult = 0.7 * (1.0 - conf)
    aot = jnp.where(inside, conf * seed + (1.0 - conf) * prior, 0.0)
    for _ in range(SWEEPS):
        near = (
            pltpu.roll(aot, 15, 0)
            + pltpu.roll(aot, 1, 0)
            + pltpu.roll(aot, 127, 1)
            + pltpu.roll(aot, 1, 1)
        )
        aot = jnp.where(inside, fix + mult * (near / count), 0.0)
    return pltpu.roll(aot, 10, 0)[0:8]


def last_kernel(
    scales, field, outer, inner, cells, far_outer, far_inner,
    far_mat, col_mat, env, halo, out, passed, result, sems,
):
    core = lax.rem(lax.axis_index("across"), 2)
    for slot in range(3):
        passed[slot, 2 * HALO : 256, :] = jnp.zeros((256 - 2 * HALO, 3 * COLS), BF16)

    lane = iota((2 * HALO, SIDE), 1)

    def last_band(strip, start):
        value = jnp.zeros((2 * HALO, SIDE), F32)
        for band in range(BANDS - 1):
            moved = pltpu.roll(strip[band].astype(F32), SIDE - KR + GROUP * band, 1)
            value = jnp.where(lane >= start + GROUP * band, moved, value)
        return value.astype(BF16)

    def columns(band):
        if band + 1 < BANDS:
            first = far_outer[band]
            second = far_inner[band]
        else:
            first = last_band(far_outer, jnp.where(core == 0, SIDE - KR, 0))
            second = last_band(far_inner, jnp.where(core == 0, 0, SIDE - KR))
        sides = jnp.concatenate(
            [jnp.where(core == 0, first, second), jnp.where(core == 0, second, first)], axis=1
        )
        for kern in range(3):
            at = slice(kern * COLS, (kern + 1) * COLS)
            value = jnp.dot(
                sides, side_matrix(col_mat, band, kern), preferred_element_type=F32
            )
            passed[band % 3, 0 : 2 * HALO, at] = (value + halo[band, :, at]).astype(BF16)

    columns(0)
    columns(1)
    small = cell_state(core, cells, field, outer, inner, far_outer, far_inner)
    block = iota((8, COLS), 1) // CB
    aot = jnp.zeros((8, COLS), F32)
    for j in range(CELL_COLS):
        aot = jnp.where(block == j, small[:, 4 + j : 5 + j], aot)
    gauss = []
    for center in (0.1, 0.35, 0.7):
        offset = aot - center
        gauss.append(jnp.exp(-(offset * offset) / 0.08))
    total = gauss[0] + gauss[1] + gauss[2]
    weights = [value / total for value in gauss]

    def copy(band):
        return pltpu.make_async_copy(result.at[band], out.at[band], sems.at[band])

    for band in range(BANDS):
        if band + 2 < BANDS:
            columns(band + 2)
        growth = jnp.exp(scales[band : band + 1, :] * aot)
        strength = scales[8 + band : 9 + band, :]
        own = (1.0 + strength) * growth
        scaled = strength * growth
        factors = [scaled * value for value in weights]
        sums = [
            env[band, :, kern * COLS : (kern + 1) * COLS]
            + jnp.dot(
                far_mat[band, kern * ROWS : (kern + 1) * ROWS, :],
                passed[band % 3, :, kern * COLS : (kern + 1) * COLS],
                preferred_element_type=F32,
            )
            for kern in range(3)
        ]
        for i in range(CELL_ROWS):
            part = slice(i * CB, (i + 1) * CB)
            value = own[i : i + 1, :] * field[band, part, :].astype(F32)
            for kern in range(3):
                value = value - factors[kern][i : i + 1, :] * sums[kern][part, :]
            result[band, part, :] = value
        copy(band).start()
    for band in range(BANDS):
        copy(band).wait()


def last_part(scales, field, outer, inner, cells, far_outer, far_inner, far_mat, col_mat, env, halo):
    flops = BANDS * 2 * (208 * 256 * 768 + 192 * 256 * 768)
    return pl.pallas_call(
        last_kernel,
        in_specs=[VMEM] * 11,
        out_specs=pl.BlockSpec(memory_space=pl.ANY),
        out_shape=jax.ShapeDtypeStruct((BANDS, ROWS, COLS), F32),
        scratch_shapes=[
            pltpu.VMEM((3, 256, 3 * COLS), BF16),
            pltpu.VMEM((BANDS, ROWS, COLS), F32),
            pltpu.SemaphoreType.DMA((BANDS,)),
        ],
        cost_estimate=pl.CostEstimate(
            flops=flops, bytes_accessed=12_000_000, transcendentals=0
        ),
        compiler_params=pltpu.CompilerParams(vmem_limit_bytes=8 << 20),
        name="last_part",
    )(
        scales, field, outer, inner, cells, far_outer, far_inner,
        far_mat, col_mat, env, halo,
    )


def body(toa, aot_seed, valid, cloud, land_class, row_taps, col_taps, tau, adjacency):
    to_early, to_late, to_outer, to_inner, cells, toa, row_taps, col_taps, scales = pack(
        toa, aot_seed, valid, cloud, land_class, row_taps, col_taps, tau, adjacency
    )
    early = exchange(to_early, 1)
    late = exchange(to_late, -1)
    outer = swap(to_outer, 1)
    inner = swap(to_inner, 0)
    near_mat, taps, col_mat = toeplitz(row_taps, col_taps)
    far_to_outer, far_to_inner, field = split(toa, early, late)
    far_outer = swap(far_to_outer, 1)
    far_inner = swap(far_to_inner, 0)
    env, halo, far_mat = own_part(field, outer, inner, near_mat, col_mat, taps)
    return last_part(
        scales, field, outer, inner, cells, far_outer, far_inner,
        far_mat, col_mat, env, halo,
    )


def solution(mesh):
    cells = P("along", "across")
    in_specs = (P(None, "along", "across"), cells, cells, cells, cells, P(), P(), P(), P())
    out_specs = P(None, "along", "across")
    return jax.shard_map(body, mesh=mesh, in_specs=in_specs, out_specs=out_specs, check_vma=False)
```
